512 devices in a mesh: genome: 32 (over x, z_lo, core), cols: 16 (over z_hi, y).
Axes of the slice: x: 4, y: 8, z: 8 (z_hi: 2, z_lo: 4; z = z_hi * 4 + z_lo), core: 2. Of those that a mesh axis runs over, the one named last changes fastest.
Arguments:
- genotypes: int32 [30720, 16384], P('cols', 'genome'), may hold values from 0 to 2
- z_scores: float32 [16384, 2944], P('genome', 'cols'), may hold values from -90 to 90
Outputs:
- effects: float32 [16384, 2944], P('genome', 'cols')
- residual: float32 [16384, 2944], P('genome', 'cols')
The draws below stay inside these ranges and needn't reach their ends.
All inputs are finite; a program needn't handle non-finite values.
Results may differ from the reference program's by a relative error of at most 0.0034.
Values may be sent and summed in bfloat16 or wider, within the bound.
No kernel may reach another device: no remote copies, remote signals or barrier semaphores. Data moves between devices by JAX's collectives and lax.ppermute only.
A program may use at most 64 MiB of HBM per device.

```python
import math
import jax
import jax.numpy as jnp
from jax import lax

MB = 512
S_DEV = 1920
W = 512
ITERS = 3
S = 30720
M = 16384
P_SIZE = 2944


def draw_genotypes(key, part):
    ld_window = 2 * W
    mean_sum = ld_window * 999 // 2
    spread_sum = int(808.0 * math.sqrt(ld_window))
    thresholds = jax.random.randint(jax.random.fold_in(key, 7), (M,), mean_sum - spread_sum, mean_sum + 1)

    def one_block(block_index):
        dosage = jnp.zeros((S_DEV, M), jnp.int32)
        for strand in range(2):
            strand_key = jax.random.fold_in(jax.random.fold_in(key, block_index), strand + 11)
            uniform_draws = jax.random.randint(strand_key, (S_DEV, M + ld_window - 1), 0, 1000)
            running = jnp.cumsum(uniform_draws, axis=1)
            shifted = jnp.pad(running, ((0, 0), (1, 0)))[:, :M]
            window = running[:, ld_window - 1:] - shifted
            dosage = dosage + (window < thresholds[None, :]).astype(jnp.int32)
        return dosage
    blocked = lax.map(one_block, jnp.arange(S // S_DEV, dtype=jnp.int32))
    return blocked.reshape(S, M)


def draw_z_scores(key, part):
    key_base = jax.random.fold_in(key, 21)
    key_rows = jax.random.fold_in(key, 22)
    key_cols = jax.random.fold_in(key, 23)
    position = jnp.arange(M, dtype=jnp.float32) / M
    rise_factor = jnp.exp(jnp.log(3.0) * position)[:, None]
    row_scale = jnp.exp(jax.random.uniform(key_rows, (M, 1), jnp.float32, 0.0, jnp.log(10.0)))
    pattern = jnp.clip(jax.random.normal(key_base, (M, P_SIZE), jnp.float32), -5.0, 5.0)
    col_scale = jnp.exp(jax.random.uniform(key_cols, (1, P_SIZE), jnp.float32, jnp.log(0.3), jnp.log(3.0)))
    return jnp.clip(0.2 * pattern * row_scale * col_scale * rise_factor, -90.0, 90.0)


def setup_inputs(seed: int = 0) -> dict:
    splits = jax.random.split(jax.random.key(seed), 3)
    genotypes = draw_genotypes(jax.random.fold_in(splits[2], 71), 0)
    z_scores = draw_z_scores(jax.random.fold_in(splits[2], 71), 0)
    return dict(genotypes=genotypes, z_scores=z_scores)


ridge_term = 0.1
floor_variance = 0.02

def tapering_table(block_rows, band_reach):
    row_index = jnp.arange(block_rows, dtype=jnp.int32)[:, None]
    col_index = jnp.arange(block_rows + 2 * band_reach, dtype=jnp.int32)[None, :]
    offset = jnp.abs(col_index - band_reach - row_index).astype(jnp.float32)
    return jnp.maximum(1.0 - offset / (band_reach + 1), 0.0)

def reference(genotypes, z_scores):
    blocked = genotypes.reshape(S, M // MB, MB).transpose(1, 0, 2)

    def standardize(block):
        dosage = block.astype(jnp.float32)
        allele_mean = lax.optimization_barrier(jnp.sum(dosage, axis=0)) / S
        variance = jnp.maximum(lax.optimization_barrier(jnp.sum(dosage * dosage, axis=0)) / S - allele_mean * allele_mean, floor_variance)
        return ((dosage - allele_mean) / jnp.sqrt(variance)).astype(jnp.bfloat16)
    standard = lax.map(standardize, blocked)
    empty = jnp.zeros((1, S, MB), jnp.bfloat16)
    padded = jnp.concatenate([empty, standard, empty], axis=0)
    tapering = tapering_table(MB, W)

    def gram_block(block_index):
        own = lax.dynamic_index_in_dim(padded, block_index + 1, 0, keepdims=False)
        before = lax.dynamic_index_in_dim(padded, block_index, 0, keepdims=False)[:, MB - W:]
        after = lax.dynamic_index_in_dim(padded, block_index + 2, 0, keepdims=False)[:, :W]
        window = jnp.concatenate([before, own, after], axis=1)
        gram = lax.dot_general(own, window, (((0,), (0,)), ((), ())), preferred_element_type=jnp.float32)
        return tapering * (gram / S)
    linkage = lax.map(gram_block, jnp.arange(M // MB, dtype=jnp.int32))

    def operate(vector):
        tall = jnp.pad(vector, ((W, W), (0, 0)))

        def product(block_index):
            window_rows = lax.dynamic_slice_in_dim(tall, block_index * MB, MB + 2 * W, 0)
            matrix = lax.dynamic_index_in_dim(linkage, block_index, 0, keepdims=False)
            return jnp.dot(matrix, window_rows, precision=lax.Precision.HIGHEST, preferred_element_type=jnp.float32)
        result = lax.map(product, jnp.arange(M // MB, dtype=jnp.int32)).reshape(M, P_SIZE)
        return result + ridge_term * vector
    effects = jnp.zeros_like(z_scores)
    residual = z_scores
    direction = z_scores
    norm_now = lax.optimization_barrier(jnp.sum(residual * residual, axis=0))
    for iteration in range(ITERS):
        image = operate(direction)
        step_size = norm_now / lax.optimization_barrier(jnp.sum(direction * image, axis=0))
        effects = effects + step_size * direction
        residual = residual - step_size * image
        norm_next = lax.optimization_barrier(jnp.sum(residual * residual, axis=0))
        direction = residual + norm_next / norm_now * direction
        norm_now = norm_next
    return (effects, residual)
```

```python
import functools

import jax
import jax.numpy as jnp
from jax import lax
from jax.experimental import pallas as pl
from jax.experimental.pallas import tpu as pltpu
from jax.sharding import PartitionSpec as P

W = 512
RIDGE = 0.1
FLOOR = 0.02
TILE = 128
SIDE = W // TILE
TILES = tuple((p, q) for p in range(SIDE) for q in range(p + 1))
NT = len(TILES)
CODE = 32000.0
f32, bf16, i16, i32 = jnp.float32, jnp.bfloat16, jnp.int16, jnp.int32


def dot(a, b):
    return jnp.dot(a, b, preferred_element_type=f32)


def halves(a):
    high = a.astype(bf16)
    return high, (a - high.astype(f32)).astype(bf16)


def call(kernel, outs, *args):
    spec = pl.BlockSpec(memory_space=pltpu.VMEM)
    scalars = [a.dtype == i32 and a.ndim == 1 for a in args]
    return pl.pallas_call(
        kernel,
        out_shape=outs,
        in_specs=[pl.BlockSpec(memory_space=pltpu.SMEM) if s else spec for s in scalars],
        out_specs=jax.tree.map(lambda _: spec, outs, is_leaf=lambda o: not isinstance(o, tuple)),
        compiler_params=pltpu.CompilerParams(vmem_limit_bytes=16 << 20),
    )(*(a if s else pltpu.with_memory_space_constraint(a, pltpu.VMEM) for a, s in zip(args, scalars)))


def shape(*dims, dtype=f32):
    return pltpu.VMEM(dims, dtype)


def pack_products(gram, block, out_ref):
    peers = out_ref.shape[0]
    rows = TILE // peers
    pieces = [
        gram[p * TILE : (p + 1) * TILE, q * TILE : (q + 1) * TILE].reshape(peers, rows, TILE) for p, q in TILES
    ]
    ones = jnp.ones((8, block.shape[0]), bf16)
    sums = dot(ones, block)[:1]
    squares = dot(ones, block * block)[:1]
    stats = [v[:, q * TILE : (q + 1) * TILE] for v in (sums, squares) for q in range(SIDE)]
    stats = jnp.concatenate(stats + [jnp.zeros((8, TILE), f32)], axis=0)
    for u in range(NT // 2):
        pair = jnp.concatenate(pieces[2 * u : 2 * u + 2], axis=1)
        out_ref[:, 2 * rows * u : 2 * rows * (u + 1), :] = pair.astype(i32).astype(i16)
    stats = stats.astype(i32).astype(i16)
    for k in range(peers):
        out_ref[k, NT * rows : NT * rows + 16, :] = stats


def own_products(x_ref, out_ref, turned_ref):
    block = x_ref[...]
    turned = block.T
    turned_ref[...] = turned
    pack_products(dot(turned, block), block, out_ref)


def next_products(turned_ref, x_ref, out_ref):
    block = x_ref[...]
    pack_products(dot(turned_ref[...], block), block, out_ref)


def correlate(samples, me_ref, own_ref, next_ref, out_ref):
    peers = own_ref.shape[0]
    rows = TILE // peers

    def total(ref):
        acc = ref[0].astype(i32)
        for k in range(1, peers):
            acc = acc + ref[k].astype(i32)
        return acc.astype(f32) / samples

    def stats(means):
        mean = means[NT * rows : NT * rows + SIDE]
        square = means[NT * rows + SIDE : NT * rows + 2 * SIDE]
        return mean, 1.0 / jnp.sqrt(jnp.maximum(square - mean * mean, FLOOR))

    own, nxt = total(own_ref), total(next_ref)
    own_stats, next_stats = stats(own), stats(nxt)
    lane = lax.broadcasted_iota(i32, (rows, TILE), 1)
    row = lax.broadcasted_iota(i32, (rows, TILE), 0) + me_ref[0] * rows

    def at_rows(vector, p):
        return jnp.sum(jnp.where(lane == row, vector[p : p + 1], 0.0), axis=1, keepdims=True)

    row_mean = [at_rows(own_stats[0], p) for p in range(SIDE)]
    row_scale = [at_rows(own_stats[1], p) * CODE for p in range(SIDE)]
    base = 0
    for means, (mean, scale) in ((own, own_stats), (nxt, next_stats)):
        codes = []
        for t, (p, q) in enumerate(TILES):
            cov = means[t * rows : (t + 1) * rows] - row_mean[p] * mean[q : q + 1]
            codes.append(jnp.round(cov * row_scale[p] * scale[q : q + 1]))
        codes = jnp.concatenate(codes, axis=0).astype(i32).astype(i16)
        for k in range(peers):
            out_ref[k, base : base + NT * rows, :] = codes
        base += NT * rows


def taper(p, q, shift):
    row = lax.broadcasted_iota(i32, (TILE, TILE), 0) + p * TILE
    col = lax.broadcasted_iota(i32, (TILE, TILE), 1) + q * TILE + shift
    reach = jnp.abs(col - row).astype(f32)
    return jnp.maximum(1.0 - reach / (W + 1), 0.0)


def unpack(codes_ref, near_high, near_low, next_high, next_low, back_high, back_low):
    peers = codes_ref.shape[0]
    rows = TILE // peers

    def tiles(base):
        for u in range(NT // 2):
            lo = base + 2 * rows * u
            pair = codes_ref[:, lo : lo + 2 * rows, :].astype(i32).astype(f32)
            yield TILES[2 * u], pair[:, :rows].reshape(TILE, TILE)
            yield TILES[2 * u + 1], pair[:, rows:].reshape(TILE, TILE)

    def put(high_ref, low_ref, p, q, value):
        high, low = halves(value)
        high_ref[p * TILE : (p + 1) * TILE, q * TILE : (q + 1) * TILE] = high
        low_ref[p * TILE : (p + 1) * TILE, q * TILE : (q + 1) * TILE] = low

    for (p, q), code in tiles(0):
        value = code * (taper(p, q, 0) * (1.0 / CODE))
        put(near_high, near_low, p, q, value)
        if p != q:
            put(near_high, near_low, q, p, value.T)
    zero = jnp.zeros((TILE, TILE), f32)
    for (p, q), code in tiles(NT * rows):
        value = code * (taper(p, q, W) * (1.0 / CODE))
        put(next_high, next_low, p, q, value)
        put(back_high, back_low, q, p, value.T)
        if p != q:
            put(next_high, next_low, q, p, zero)
            put(back_high, back_low, p, q, zero)


def product(v, high_ref, low_ref):
    high, low = halves(v)
    return dot(high, high_ref[...]) + dot(low, high_ref[...]) + dot(high, low_ref[...])


def outward(v_ref, high_ref, low_ref, out_ref):
    out_ref[...] = product(v_ref[...], high_ref, low_ref)


def inward(v_ref, high_ref, low_ref, out_ref):
    out_ref[...] = product(v_ref[...], high_ref, low_ref) + RIDGE * v_ref[...]


def gather_in(part_ref, came_ref, next_ref, high_ref, low_ref, out_ref):
    out_ref[...] = part_ref[...] + came_ref[...] + product(next_ref[...], high_ref, low_ref)


def along(a, b):
    return jnp.sum(a * b, axis=1, keepdims=True)


def early_moments(a_ref, b_ref, c_ref, out_ref):
    a, b, c = a_ref[...], b_ref[...], c_ref[...]
    lane = lax.broadcasted_iota(i32, out_ref.shape, 1)
    total = jnp.zeros(out_ref.shape, f32)
    for k, m in enumerate((along(a, a), along(a, b), along(b, b), along(b, c), along(c, c))):
        total = jnp.where(lane == k, m, total)
    out_ref[...] = total


def last_vector(part_ref, came_ref, next_ref, high_ref, low_ref, c_ref, early_ref, out_ref, moments_ref):
    w = part_ref[...] + came_ref[...] + product(next_ref[...], high_ref, low_ref)
    out_ref[...] = w
    lane = lax.broadcasted_iota(i32, early_ref.shape, 1)
    total = jnp.where(lane == 5, along(c_ref[...], w), early_ref[...])
    fill = moments_ref.shape[2] - total.shape[0]
    turned = jnp.concatenate([total, jnp.zeros((fill, TILE), f32)], axis=0).T[:8]
    for k in range(moments_ref.shape[0]):
        moments_ref[k] = turned


def combine(moments_ref, a_ref, b_ref, c_ref, d_ref, effects_ref, residual_ref):
    total = moments_ref[0]
    for k in range(1, moments_ref.shape[0]):
        total = total + moments_ref[k]
    moment = [total[k : k + 1] / total[:1] for k in range(6)]

    def inner(x, y, power):
        return sum(
            x[i] * y[j] * moment[i + j + power] for i in range(len(x)) for j in range(len(y))
        )

    one = jnp.ones_like(moment[0])
    residual, direction, effects = [one], [one], []
    norm_now = inner(residual, residual, 0)
    for step in range(3):
        step_size = norm_now / inner(direction, direction, 1)
        effects = [
            (effects[k] if k < len(effects) else 0.0) + step_size * direction[k] for k in range(len(direction))
        ]
        image = [0.0] + direction
        residual = [
            (residual[k] if k < len(residual) else 0.0) - step_size * image[k] for k in range(len(image))
        ]
        if step < 2:
            norm_next = inner(residual, residual, 0)
            ratio = norm_next / norm_now
            direction = [
                residual[k] + (ratio * direction[k] if k < len(direction) else 0.0) for k in range(len(residual))
            ]
            norm_now = norm_next
    rows = effects + residual
    table = jnp.concatenate(rows + [jnp.zeros((TILE - len(rows), total.shape[1]), f32)], axis=0).T
    table = table[: a_ref.shape[0]]
    col = [table[:, k : k + 1] for k in range(len(rows))]
    a, b, c, d = a_ref[...], b_ref[...], c_ref[...], d_ref[...]
    effects_ref[...] = col[0] * a + col[1] * b + col[2] * c
    residual_ref[...] = col[3] * a + col[4] * b + col[5] * c + col[6] * d


def shards(genotypes, z_scores):
    local_samples, variants = genotypes.shape
    blocks = lax.axis_size("genome")
    peers = lax.axis_size("cols")
    samples = local_samples * peers
    to_left = [(k + 1, k) for k in range(blocks - 1)]
    to_right = [(k, k + 1) for k in range(blocks - 1)]
    rows = TILE // peers

    dosage = genotypes.astype(bf16)
    next_dosage = lax.ppermute(dosage, "genome", to_left)
    packed = shape(peers, NT * rows + 16, TILE, dtype=i16)
    own, turned = call(own_products, (packed, shape(variants, local_samples, dtype=bf16)), dosage)
    own = lax.all_to_all(own, "cols", 0, 0)
    own, next_dosage = lax.optimization_barrier((own, next_dosage))
    nxt = call(next_products, packed, turned, next_dosage)
    z = z_scores.T
    z, nxt = lax.optimization_barrier((z, nxt))
    z_next = lax.ppermute(z, "genome", to_left)
    nxt = lax.all_to_all(nxt, "cols", 0, 0)
    me = lax.axis_index("cols").astype(i32).reshape(1)
    codes = call(functools.partial(correlate, samples), shape(peers, 2 * NT * rows, TILE, dtype=i16), me, own, nxt)
    codes = lax.all_to_all(codes, "cols", 0, 0)
    square = shape(W, W, dtype=bf16)
    near_h, near_l, next_h, next_l, back_h, back_l = call(unpack, (square,) * 6, codes)

    vector = shape(*z.shape)

    def spread(v):
        came = lax.ppermute(call(outward, vector, v, next_h, next_l), "genome", to_right)
        return came, call(inward, vector, v, near_h, near_l)

    came, part = spread(z)
    one = call(gather_in, vector, part, came, z_next, back_h, back_l)
    one_next = lax.ppermute(one, "genome", to_left)
    came, part = spread(one)
    two = call(gather_in, vector, part, came, one_next, back_h, back_l)
    two_next = lax.ppermute(two, "genome", to_left)
    came, part = spread(two)
    early = call(early_moments, shape(z.shape[0], TILE), z, one, two)
    three, moments = call(
        last_vector, (vector, shape(blocks, 8, 256)), part, came, two_next, back_h, back_l, two, early
    )
    moments = lax.all_to_all(moments, "genome", 0, 0)
    effects, residual = call(combine, (jax.ShapeDtypeStruct(z.shape, f32),) * 2, moments, z, one, two, three)
    return effects.T, residual.T


def solution(mesh):
    return jax.shard_map(
        shards,
        mesh=mesh,
        in_specs=(P("cols", "genome"), P("genome", "cols")),
        out_specs=(P("genome", "cols"), P("genome", "cols")),
        check_vma=False,
    )
```

```python
import functools

import jax
import jax.numpy as jnp
from jax import lax
from jax.experimental import pallas as pl
from jax.experimental.pallas import tpu as pltpu
from jax.sharding import PartitionSpec as P

W = 512
RIDGE = 0.1
FLOOR = 0.02
TILE = 128
SIDE = W // TILE
TILES = tuple((p, q) for p in range(SIDE) for q in range(p + 1))
NT = len(TILES)
CODE = 32000.0
HALF = 32768
f32, bf16, i16, i32 = jnp.float32, jnp.bfloat16, jnp.int16, jnp.int32


def dot(a, b):
    return jnp.dot(a, b, preferred_element_type=f32)


def halves(a):
    high = a.astype(bf16)
    return high, (a - high.astype(f32)).astype(bf16)


def call(kernel, outs, *args):
    spec = pl.BlockSpec(memory_space=pltpu.VMEM)
    scalars = [a.dtype == i32 and a.ndim == 1 for a in args]
    return pl.pallas_call(
        kernel,
        out_shape=outs,
        in_specs=[pl.BlockSpec(memory_space=pltpu.SMEM) if s else spec for s in scalars],
        out_specs=jax.tree.map(lambda _: spec, outs, is_leaf=lambda o: not isinstance(o, tuple)),
        compiler_params=pltpu.CompilerParams(vmem_limit_bytes=16 << 20),
    )(*(a if s else pltpu.with_memory_space_constraint(a, pltpu.VMEM) for a, s in zip(args, scalars)))


def shape(*dims, dtype=f32):
    return pltpu.VMEM(dims, dtype)


def pack_products(gram, block, put, peers):
    rows = TILE // peers
    pieces = [
        gram[p * TILE : (p + 1) * TILE, q * TILE : (q + 1) * TILE].reshape(peers, rows, TILE) for p, q in TILES
    ]
    ones = jnp.ones((8, block.shape[0]), bf16)
    sums = dot(ones, block)[:1]
    squares = dot(ones, block * block)[:1]
    stats = [v[:, q * TILE : (q + 1) * TILE] for v in (sums, squares) for q in range(SIDE)]
    stats = jnp.concatenate(stats + [jnp.zeros((8, TILE), f32)], axis=0)
    for u in range(NT // 2):
        pair = jnp.concatenate(pieces[2 * u : 2 * u + 2], axis=1)
        put(2 * rows * u, pair.astype(i32).astype(i16))
    stats = jnp.broadcast_to(stats.astype(i32).astype(i16)[None], (peers, *stats.shape))
    put(NT * rows, stats)


def own_products(x_ref, out_ref, turned_ref):
    block = x_ref[...]
    turned = block.T
    turned_ref[...] = turned
    near, depth = out_ref.shape[0], out_ref.shape[1] // 2

    def put(at, value):
        for far in range(2):
            lo = far * depth + at
            out_ref[:, lo : lo + value.shape[1], :] = value[far * near : (far + 1) * near]

    pack_products(dot(turned, block), block, put, 2 * near)


def next_products(turned_ref, x_ref, out_ref):
    block = x_ref[...]

    def put(at, value):
        out_ref[:, at : at + value.shape[1], :] = value

    pack_products(dot(turned_ref[...], block), block, put, out_ref.shape[0])


def fold(me_ref, came_ref, keep_ref, send_ref):
    near, depth = came_ref.shape[0], came_ref.shape[1] // 2
    far = me_ref[0] // near

    def total(side):
        rows = pl.ds(pl.multiple_of(side * depth, depth), depth)
        acc = came_ref[0, rows, :].astype(i32)
        for k in range(1, near):
            acc = acc + came_ref[k, rows, :].astype(i32)
        return acc

    keep_ref[...] = total(far)
    send_ref[...] = (total(1 - far) - HALF).astype(i16)


def correlate(samples, me_ref, keep_ref, far_ref, next_ref, out_ref):
    peers = next_ref.shape[0]
    rows = TILE // peers

    def stats(means):
        mean = means[NT * rows : NT * rows + SIDE]
        square = means[NT * rows + SIDE : NT * rows + 2 * SIDE]
        return mean, 1.0 / jnp.sqrt(jnp.maximum(square - mean * mean, FLOOR))

    own = keep_ref[...] + far_ref[...].astype(i32) + HALF
    nxt = next_ref[0].astype(i32)
    for k in range(1, peers):
        nxt = nxt + next_ref[k].astype(i32)
    own, nxt = own.astype(f32) / samples, nxt.astype(f32) / samples
    own_stats, next_stats = stats(own), stats(nxt)
    lane = lax.broadcasted_iota(i32, (rows, TILE), 1)
    row = lax.broadcasted_iota(i32, (rows, TILE), 0) + me_ref[0] * rows

    def at_rows(vector, p):
        return jnp.sum(jnp.where(lane == row, vector[p : p + 1], 0.0), axis=1, keepdims=True)

    row_mean = [at_rows(own_stats[0], p) for p in range(SIDE)]
    row_scale = [at_rows(own_stats[1], p) * CODE for p in range(SIDE)]
    base = 0
    for means, (mean, scale) in ((own, own_stats), (nxt, next_stats)):
        codes = []
        for t, (p, q) in enumerate(TILES):
            cov = means[t * rows : (t + 1) * rows] - row_mean[p] * mean[q : q + 1]
            codes.append(jnp.round(cov * row_scale[p] * scale[q : q + 1]))
        codes = jnp.concatenate(codes, axis=0).astype(i32).astype(i16)
        for k in range(peers):
            out_ref[k, base : base + NT * rows, :] = codes
        base += NT * rows


def taper(p, q, shift):
    row = lax.broadcasted_iota(i32, (TILE, TILE), 0) + p * TILE
    col = lax.broadcasted_iota(i32, (TILE, TILE), 1) + q * TILE + shift
    reach = jnp.abs(col - row).astype(f32)
    return jnp.maximum(1.0 - reach / (W + 1), 0.0)


def unpack(codes_ref, near_high, near_low, next_high, next_low, back_high, back_low):
    peers = codes_ref.shape[0]
    rows = TILE // peers

    def tiles(base):
        for u in range(NT // 2):
            lo = base + 2 * rows * u
            pair = codes_ref[:, lo : lo + 2 * rows, :].astype(i32).astype(f32)
            yield TILES[2 * u], pair[:, :rows].reshape(TILE, TILE)
            yield TILES[2 * u + 1], pair[:, rows:].reshape(TILE, TILE)

    def put(high_ref, low_ref, p, q, value):
        high, low = halves(value)
        high_ref[p * TILE : (p + 1) * TILE, q * TILE : (q + 1) * TILE] = high
        low_ref[p * TILE : (p + 1) * TILE, q * TILE : (q + 1) * TILE] = low

    for (p, q), code in tiles(0):
        value = code * (taper(p, q, 0) * (1.0 / CODE))
        put(near_high, near_low, p, q, value)
        if p != q:
            put(near_high, near_low, q, p, value.T)
    zero = jnp.zeros((TILE, TILE), f32)
    for (p, q), code in tiles(NT * rows):
        value = code * (taper(p, q, W) * (1.0 / CODE))
        put(next_high, next_low, p, q, value)
        put(back_high, back_low, q, p, value.T)
        if p != q:
            put(next_high, next_low, q, p, zero)
            put(back_high, back_low, p, q, zero)


def product(v, high_ref, low_ref):
    high, low = halves(v)
    return dot(high, high_ref[...]) + dot(low, high_ref[...]) + dot(high, low_ref[...])


def diagonal(rows):
    return lax.broadcasted_iota(i32, (rows, 256), 0) == lax.broadcasted_iota(i32, (rows, 256), 1)


def encode(v, out_ref):
    rows = v.shape[0]
    top = jnp.max(jnp.abs(v), axis=1, keepdims=True)
    power = jnp.ceil(jnp.log2(jnp.maximum(top, 1e-30)) + 0.01)
    code = jnp.round(v * (jnp.exp2(-power) * CODE))
    turned = jnp.sum(jnp.where(diagonal(rows), power, 0.0), axis=0, keepdims=True)
    tail = jnp.broadcast_to(jnp.concatenate([turned, turned], axis=1), (out_ref.shape[0] - rows, v.shape[1]))
    out_ref[...] = jnp.concatenate([code, tail], axis=0).astype(i32).astype(i16)


def decode(code_ref, rows):
    code = code_ref[...].astype(i32).astype(f32)
    power = jnp.sum(jnp.where(diagonal(rows), code[rows : rows + 1, :256], 0.0), axis=1, keepdims=True)
    return code[:rows] * (jnp.exp2(power) * (1.0 / CODE))


def start_code(v_ref, out_ref):
    encode(v_ref[...], out_ref)


def outward(v_ref, high_ref, low_ref, out_ref):
    encode(product(v_ref[...], high_ref, low_ref), out_ref)


def inward(v_ref, high_ref, low_ref, out_ref):
    out_ref[...] = product(v_ref[...], high_ref, low_ref) + RIDGE * v_ref[...]


def gather(part_ref, came_ref, next_ref, high_ref, low_ref):
    rows = part_ref.shape[0]
    return part_ref[...] + decode(came_ref, rows) + product(decode(next_ref, rows), high_ref, low_ref)


def gather_in(part_ref, came_ref, next_ref, back_h, back_l, next_h, next_l, out_ref, left_ref, right_ref):
    w = gather(part_ref, came_ref, next_ref, back_h, back_l)
    out_ref[...] = w
    encode(w, left_ref)
    encode(product(w, next_h, next_l), right_ref)


def along(a, b):
    return jnp.sum(a * b, axis=1, keepdims=True)


def turn(moment):
    return jnp.sum(jnp.where(diagonal(moment.shape[0]), moment, 0.0), axis=0, keepdims=True)


def early_moments(a_ref, b_ref, c_ref, out_ref):
    a, b, c = a_ref[...], b_ref[...], c_ref[...]
    rows = [turn(m) for m in (along(a, a), along(a, b), along(b, b), along(b, c), along(c, c))]
    out_ref[...] = jnp.concatenate(rows + [jnp.zeros((3, 256), f32)], axis=0)


def last_vector(part_ref, came_ref, next_ref, back_h, back_l, c_ref, early_ref, out_ref, moments_ref):
    w = gather(part_ref, came_ref, next_ref, back_h, back_l)
    out_ref[...] = w
    row = lax.broadcasted_iota(i32, early_ref.shape, 0)
    moments = jnp.where(row == 5, turn(along(c_ref[...], w)), early_ref[...])
    for k in range(moments_ref.shape[0]):
        moments_ref[k] = moments


def combine(moments_ref, a_ref, b_ref, c_ref, d_ref, effects_ref, residual_ref):
    total = moments_ref[0]
    for k in range(1, moments_ref.shape[0]):
        total = total + moments_ref[k]
    moment = [total[k : k + 1] / total[:1] for k in range(6)]

    def inner(x, y, power):
        return sum(
            x[i] * y[j] * moment[i + j + power] for i in range(len(x)) for j in range(len(y))
        )

    one = jnp.ones_like(moment[0])
    residual, direction, effects = [one], [one], []
    norm_now = inner(residual, residual, 0)
    for step in range(3):
        step_size = norm_now / inner(direction, direction, 1)
        effects = [
            (effects[k] if k < len(effects) else 0.0) + step_size * direction[k] for k in range(len(direction))
        ]
        image = [0.0] + direction
        residual = [
            (residual[k] if k < len(residual) else 0.0) - step_size * image[k] for k in range(len(image))
        ]
        if step < 2:
            norm_next = inner(residual, residual, 0)
            ratio = norm_next / norm_now
            direction = [
                residual[k] + (ratio * direction[k] if k < len(direction) else 0.0) for k in range(len(residual))
            ]
            norm_now = norm_next
    rows = effects + residual
    table = jnp.concatenate(rows + [jnp.zeros((TILE - len(rows), total.shape[1]), f32)], axis=0).T
    table = table[: a_ref.shape[0]]
    col = [table[:, k : k + 1] for k in range(len(rows))]
    a, b, c, d = a_ref[...], b_ref[...], c_ref[...], d_ref[...]
    effects_ref[...] = col[0] * a + col[1] * b + col[2] * c
    residual_ref[...] = col[3] * a + col[4] * b + col[5] * c + col[6] * d


def shards(genotypes, z_scores):
    local_samples, variants = genotypes.shape
    blocks = lax.axis_size("genome")
    peers = lax.axis_size("cols")
    samples = local_samples * peers
    to_left = [(k + 1, k) for k in range(blocks - 1)]
    to_right = [(k, k + 1) for k in range(blocks - 1)]
    rows = TILE // peers

    near = peers // 2
    depth = NT * rows + 16
    cols = range(peers)
    sides = [list(cols[:near]), list(cols[near:])]

    dosage = genotypes.astype(bf16)
    next_dosage = lax.ppermute(dosage, "genome", to_left)
    own, turned = call(
        own_products,
        (shape(near, 2 * depth, TILE, dtype=i16), shape(variants, local_samples, dtype=bf16)),
        dosage,
    )
    own = lax.all_to_all(own, "cols", 0, 0, axis_index_groups=sides)
    me = lax.axis_index("cols").astype(i32).reshape(1)
    keep, far = call(fold, (shape(depth, TILE, dtype=i32), shape(depth, TILE, dtype=i16)), me, own)
    far = lax.ppermute(far, "cols", [(k, (k + near) % peers) for k in cols])
    z = z_scores.T
    vector = shape(*z.shape)
    code = shape(z.shape[0] // 16 * 16 + 16, z.shape[1], dtype=i16)
    z_code = call(start_code, code, z)
    far, next_dosage, z_code = lax.optimization_barrier((far, next_dosage, z_code))
    nxt = call(next_products, shape(peers, depth, TILE, dtype=i16), turned, next_dosage)
    z_code, nxt = lax.optimization_barrier((z_code, nxt))
    nxt = lax.all_to_all(nxt, "cols", 0, 0)
    z_next = lax.ppermute(z_code, "genome", to_left)
    codes = call(
        functools.partial(correlate, samples), shape(peers, 2 * NT * rows, TILE, dtype=i16), me, keep, far, nxt
    )
    codes = lax.all_to_all(codes, "cols", 0, 0)
    square = shape(W, W, dtype=bf16)
    near_h, near_l, next_h, next_l, back_h, back_l = call(unpack, (square,) * 6, codes)

    def step(part, came, nxt):
        w, left, right = call(
            gather_in, (vector, code, code), part, came, nxt, back_h, back_l, next_h, next_l
        )
        came = lax.ppermute(right, "genome", to_right)
        nxt = lax.ppermute(left, "genome", to_left)
        return w, came, nxt, call(inward, vector, w, near_h, near_l)

    came = lax.ppermute(call(outward, code, z, next_h, next_l), "genome", to_right)
    one, came, nxt, part = step(call(inward, vector, z, near_h, near_l), came, z_next)
    two, came, nxt, part = step(part, came, nxt)
    early = call(early_moments, shape(8, 256), z, one, two)
    three, moments = call(
        last_vector, (vector, shape(blocks, 8, 256)), part, came, nxt, back_h, back_l, two, early
    )
    moments = lax.all_to_all(moments, "genome", 0, 0)
    effects, residual = call(combine, (jax.ShapeDtypeStruct(z.shape, f32),) * 2, moments, z, one, two, three)
    return effects.T, residual.T


def solution(mesh):
    return jax.shard_map(
        shards,
        mesh=mesh,
        in_specs=(P("cols", "genome"), P("genome", "cols")),
        out_specs=(P("genome", "cols"), P("genome", "cols")),
        check_vma=False,
    )
```

```python
import functools

import jax
import jax.numpy as jnp
from jax import lax
from jax.experimental import pallas as pl
from jax.experimental.pallas import tpu as pltpu
from jax.sharding import PartitionSpec as P

W = 512
RIDGE = 0.1
FLOOR = 0.02
TILE = 128
SIDE = W // TILE
UPPER = tuple((p, q) for p in range(SIDE) for q in range(p, SIDE))
LOWER = tuple((p, q) for p in range(SIDE) for q in range(p + 1))
NT = len(UPPER)
CODE = 32000.0
HALF = 32768
f32, bf16, i16, i32 = jnp.float32, jnp.bfloat16, jnp.int16, jnp.int32


def dot(a, b):
    return jnp.dot(a, b, preferred_element_type=f32)


def halves(a):
    high = a.astype(bf16)
    return high, (a - high.astype(f32)).astype(bf16)


def call(kernel, outs, *args):
    spec = pl.BlockSpec(memory_space=pltpu.VMEM)
    scalars = [a.dtype == i32 and a.ndim == 1 for a in args]
    return pl.pallas_call(
        kernel,
        out_shape=outs,
        in_specs=[pl.BlockSpec(memory_space=pltpu.SMEM) if s else spec for s in scalars],
        out_specs=jax.tree.map(lambda _: spec, outs, is_leaf=lambda o: not isinstance(o, tuple)),
        compiler_params=pltpu.CompilerParams(vmem_limit_bytes=16 << 20),
    )(*(a if s else pltpu.with_memory_space_constraint(a, pltpu.VMEM) for a, s in zip(args, scalars)))


def shape(*dims, dtype=f32):
    return pltpu.VMEM(dims, dtype)


def tile_of(matrix, p, q):
    return matrix[p * TILE : (p + 1) * TILE, q * TILE : (q + 1) * TILE]


def pack_tiles(gram, tiles, put, peers):
    rows = TILE // peers
    pieces = [tile_of(gram, p, q).reshape(peers, rows, TILE) for p, q in tiles]
    for u in range(len(tiles) // 2):
        pair = jnp.concatenate(pieces[2 * u : 2 * u + 2], axis=1)
        put(2 * rows * u, pair.astype(i32).astype(i16))


def products(left, right):
    return lax.dot_general(left, right, (((0,), (0,)), ((), ())), preferred_element_type=f32)


def on_diagonal():
    return lax.broadcasted_iota(i32, (TILE, TILE), 0) == lax.broadcasted_iota(i32, (TILE, TILE), 1)


def own_products(x_ref, out_ref):
    block = x_ref[...]
    near, depth = out_ref.shape[0], out_ref.shape[1] // 2
    peers = 2 * near

    def put(at, value):
        for far in range(2):
            lo = far * depth + at
            out_ref[:, lo : lo + value.shape[1], :] = value[far * near : (far + 1) * near]

    gram = products(block, block)
    pack_tiles(gram, UPPER, put, peers)
    sums = dot(jnp.ones((8, block.shape[0]), bf16), block)[:1]
    here = on_diagonal()
    stats = [sums[:, q * TILE : (q + 1) * TILE] for q in range(SIDE)]
    stats += [jnp.sum(jnp.where(here, tile_of(gram, q, q), 0.0), axis=0, keepdims=True) for q in range(SIDE)]
    stats = jnp.concatenate(stats + [jnp.zeros((8, TILE), f32)], axis=0)
    put(NT * TILE // peers, jnp.broadcast_to(stats.astype(i32).astype(i16)[None], (peers, 16, TILE)))


def next_products(x_ref, next_ref, out_ref):
    def put(at, value):
        out_ref[:, at : at + value.shape[1], :] = value

    pack_tiles(products(x_ref[...], next_ref[...]), LOWER, put, out_ref.shape[0])


def fold(me_ref, came_ref, keep_ref, send_ref):
    near, depth = came_ref.shape[0], came_ref.shape[1] // 2
    far = me_ref[0] // near

    def total(side):
        rows = pl.ds(pl.multiple_of(side * depth, depth), depth)
        acc = came_ref[0, rows, :].astype(i32)
        for k in range(1, near):
            acc = acc + came_ref[k, rows, :].astype(i32)
        return acc

    keep_ref[...] = total(far)
    send_ref[...] = (total(1 - far) - HALF).astype(i16)


def correlate(samples, me_ref, keep_ref, far_ref, stats_ref, next_ref, out_ref, diagonal_ref):
    peers = next_ref.shape[0]
    rows = TILE // peers
    own = keep_ref[...] + far_ref[...].astype(i32) + HALF
    nxt = next_ref[0].astype(i32)
    for k in range(1, peers):
        nxt = nxt + next_ref[k].astype(i32)
    own, nxt = own.astype(f32) / samples, nxt.astype(f32) / samples

    def stats(means):
        mean, square = means[:SIDE], means[SIDE : 2 * SIDE]
        variance = square - mean * mean
        return mean, variance, 1.0 / jnp.sqrt(jnp.maximum(variance, FLOOR))

    mean, variance, scale = stats(own[NT * rows :])
    next_mean, _, next_scale = stats(stats_ref[...].astype(f32) / samples)
    diagonal_ref[...] = jnp.concatenate([variance * scale * scale, jnp.zeros((8 - SIDE, TILE), f32)], axis=0)
    lane = lax.broadcasted_iota(i32, (rows, TILE), 1)
    row = lax.broadcasted_iota(i32, (rows, TILE), 0) + me_ref[0] * rows

    def at_rows(vector, p):
        return jnp.sum(jnp.where(lane == row, vector[p : p + 1], 0.0), axis=1, keepdims=True)

    row_mean = [at_rows(mean, p) for p in range(SIDE)]
    row_scale = [at_rows(scale, p) * CODE for p in range(SIDE)]

    def code(means, t, p, q, col_mean, col_scale):
        cov = means[t * rows : (t + 1) * rows] - row_mean[p] * col_mean[q : q + 1]
        return jnp.round(cov * row_scale[p] * col_scale[q : q + 1])

    upper = {(p, q): code(own, t, p, q, mean, scale) for t, (p, q) in enumerate(UPPER)}
    lower = {(p, q): code(nxt, t, p, q, next_mean, next_scale) for t, (p, q) in enumerate(LOWER)}
    codes = []
    for p in range(SIDE):
        for q in range(SIDE):
            if p == q:
                codes.append(jnp.where(lane > row, upper[p, q], lower[p, q]))
            else:
                codes.append(upper[p, q] if p < q else lower[p, q])
    codes = jnp.concatenate(codes, axis=0).astype(i32).astype(i16)
    for k in range(peers):
        out_ref[k] = codes


def taper(p, q, shift):
    row = lax.broadcasted_iota(i32, (TILE, TILE), 0) + p * TILE
    col = lax.broadcasted_iota(i32, (TILE, TILE), 1) + q * TILE + shift
    reach = jnp.abs(col - row).astype(f32)
    return jnp.maximum(1.0 - reach / (W + 1), 0.0)


def unpack(codes_ref, diagonal_ref, near_high, near_low, next_high, next_low, back_high, back_low):
    peers = codes_ref.shape[0]
    rows = TILE // peers

    def put(high_ref, low_ref, p, q, value):
        high, low = halves(value)
        high_ref[p * TILE : (p + 1) * TILE, q * TILE : (q + 1) * TILE] = high
        low_ref[p * TILE : (p + 1) * TILE, q * TILE : (q + 1) * TILE] = low

    def put_near(p, q, code):
        value = code * (taper(p, q, 0) * (1.0 / CODE))
        if p == q:
            value = value + value.T
            value = jnp.where(on_diagonal(), diagonal_ref[p : p + 1, :], value)
            put(near_high, near_low, p, q, value)
        else:
            put(near_high, near_low, p, q, value)
            put(near_high, near_low, q, p, value.T)

    def put_next(p, q, code):
        value = code * (taper(p, q, W) * (1.0 / CODE))
        put(next_high, next_low, p, q, value)
        put(back_high, back_low, q, p, value.T)

    strict = lax.broadcasted_iota(i32, (TILE, TILE), 0) < lax.broadcasted_iota(i32, (TILE, TILE), 1)
    zero = jnp.zeros((TILE, TILE), f32)
    for p in range(SIDE):
        for u in range(SIDE // 2):
            lo = 2 * rows * (p * SIDE // 2 + u)
            pair = codes_ref[:, lo : lo + 2 * rows, :].astype(i32).astype(f32)
            for q, code in ((2 * u, pair[:, :rows]), (2 * u + 1, pair[:, rows:])):
                code = code.reshape(TILE, TILE)
                if p <= q:
                    put_near(p, q, jnp.where(strict, code, 0.0) if p == q else code)
                if p >= q:
                    put_next(p, q, code)
                else:
                    put(next_high, next_low, p, q, zero)
                    put(back_high, back_low, q, p, zero)


def product(v, high_ref, low_ref):
    high, low = halves(v)
    return dot(high, high_ref[...]) + dot(low, high_ref[...]) + dot(high, low_ref[...])


def diagonal(rows):
    return lax.broadcasted_iota(i32, (rows, 256), 0) == lax.broadcasted_iota(i32, (rows, 256), 1)


def encode(v, out_ref):
    rows = v.shape[0]
    top = jnp.max(jnp.abs(v), axis=1, keepdims=True)
    power = jnp.ceil(jnp.log2(jnp.maximum(top, 1e-30)) + 0.01)
    code = jnp.round(v * (jnp.exp2(-power) * CODE))
    turned = jnp.sum(jnp.where(diagonal(rows), power, 0.0), axis=0, keepdims=True)
    tail = jnp.broadcast_to(jnp.concatenate([turned, turned], axis=1), (out_ref.shape[0] - rows, v.shape[1]))
    out_ref[...] = jnp.concatenate([code, tail], axis=0).astype(i32).astype(i16)


def decode(code_ref, rows):
    code = code_ref[...].astype(i32).astype(f32)
    power = jnp.sum(jnp.where(diagonal(rows), code[rows : rows + 1, :256], 0.0), axis=1, keepdims=True)
    return code[:rows] * (jnp.exp2(power) * (1.0 / CODE))


def start_code(v_ref, out_ref):
    encode(v_ref[...], out_ref)


def outward(v_ref, high_ref, low_ref, out_ref):
    encode(product(v_ref[...], high_ref, low_ref), out_ref)


def inward(v_ref, high_ref, low_ref, out_ref):
    out_ref[...] = product(v_ref[...], high_ref, low_ref) + RIDGE * v_ref[...]


def gather(part_ref, came_ref, next_ref, high_ref, low_ref):
    rows = part_ref.shape[0]
    return part_ref[...] + decode(came_ref, rows) + product(decode(next_ref, rows), high_ref, low_ref)


def gather_in(part_ref, came_ref, next_ref, back_h, back_l, next_h, next_l, out_ref, left_ref, right_ref):
    w = gather(part_ref, came_ref, next_ref, back_h, back_l)
    out_ref[...] = w
    encode(w, left_ref)
    encode(product(w, next_h, next_l), right_ref)


def along(a, b):
    return jnp.sum(a * b, axis=1, keepdims=True)


def turn(moment):
    return jnp.sum(jnp.where(diagonal(moment.shape[0]), moment, 0.0), axis=0, keepdims=True)


def early_moments(a_ref, b_ref, c_ref, out_ref):
    a, b, c = a_ref[...], b_ref[...], c_ref[...]
    rows = [turn(m) for m in (along(a, a), along(a, b), along(b, b), along(b, c), along(c, c))]
    out_ref[...] = jnp.concatenate(rows + [jnp.zeros((3, 256), f32)], axis=0)


def last_vector(part_ref, came_ref, next_ref, back_h, back_l, c_ref, early_ref, out_ref, moments_ref):
    w = gather(part_ref, came_ref, next_ref, back_h, back_l)
    out_ref[...] = w
    row = lax.broadcasted_iota(i32, early_ref.shape, 0)
    moments = jnp.where(row == 5, turn(along(c_ref[...], w)), early_ref[...])
    for k in range(moments_ref.shape[0]):
        moments_ref[k] = moments


def combine(moments_ref, a_ref, b_ref, c_ref, d_ref, effects_ref, residual_ref):
    total = moments_ref[0]
    for k in range(1, moments_ref.shape[0]):
        total = total + moments_ref[k]
    moment = [total[k : k + 1] / total[:1] for k in range(6)]

    def inner(x, y, power):
        return sum(
            x[i] * y[j] * moment[i + j + power] for i in range(len(x)) for j in range(len(y))
        )

    one = jnp.ones_like(moment[0])
    residual, direction, effects = [one], [one], []
    norm_now = inner(residual, residual, 0)
    for step in range(3):
        step_size = norm_now / inner(direction, direction, 1)
        effects = [
            (effects[k] if k < len(effects) else 0.0) + step_size * direction[k] for k in range(len(direction))
        ]
        image = [0.0] + direction
        residual = [
            (residual[k] if k < len(residual) else 0.0) - step_size * image[k] for k in range(len(image))
        ]
        if step < 2:
            norm_next = inner(residual, residual, 0)
            ratio = norm_next / norm_now
            direction = [
                residual[k] + (ratio * direction[k] if k < len(direction) else 0.0) for k in range(len(residual))
            ]
            norm_now = norm_next
    rows = effects + residual
    table = jnp.concatenate(rows + [jnp.zeros((TILE - len(rows), total.shape[1]), f32)], axis=0).T
    table = table[: a_ref.shape[0]]
    col = [table[:, k : k + 1] for k in range(len(rows))]
    a, b, c, d = a_ref[...], b_ref[...], c_ref[...], d_ref[...]
    effects_ref[...] = col[0] * a + col[1] * b + col[2] * c
    residual_ref[...] = col[3] * a + col[4] * b + col[5] * c + col[6] * d


def shards(genotypes, z_scores):
    local_samples, variants = genotypes.shape
    blocks = lax.axis_size("genome")
    peers = lax.axis_size("cols")
    samples = local_samples * peers
    to_left = [(k + 1, k) for k in range(blocks - 1)]
    to_right = [(k, k + 1) for k in range(blocks - 1)]
    rows = TILE // peers

    near = peers // 2
    depth = NT * rows + 16
    cols = range(peers)
    sides = [list(cols[:near]), list(cols[near:])]

    dosage = genotypes.astype(bf16)
    next_dosage = lax.ppermute(dosage, "genome", to_left)
    own = call(own_products, shape(near, 2 * depth, TILE, dtype=i16), dosage)
    own = lax.all_to_all(own, "cols", 0, 0, axis_index_groups=sides)
    me = lax.axis_index("cols").astype(i32).reshape(1)
    keep, far = call(fold, (shape(depth, TILE, dtype=i32), shape(depth, TILE, dtype=i16)), me, own)
    z = z_scores.T
    vector = shape(*z.shape)
    code = shape(z.shape[0] // 16 * 16 + 16, z.shape[1], dtype=i16)
    z_code = call(start_code, code, z)
    keep, next_dosage = lax.optimization_barrier((keep, next_dosage))
    nxt = call(next_products, shape(peers, NT * rows, TILE, dtype=i16), dosage, next_dosage)
    far, z_code, nxt = lax.optimization_barrier((far, z_code, nxt))
    nxt = lax.all_to_all(nxt, "cols", 0, 0)
    far = lax.ppermute(far, "cols", [(k, (k + near) % peers) for k in cols])
    stats = keep[NT * rows : NT * rows + 8] + far[NT * rows : NT * rows + 8].astype(i32) + HALF
    next_stats = lax.ppermute(stats, "genome", to_left)
    z_next = lax.ppermute(z_code, "genome", to_left)
    codes, diagonal_row = call(
        functools.partial(correlate, samples),
        (shape(peers, SIDE * SIDE * rows, TILE, dtype=i16), shape(8, TILE)),
        me,
        keep,
        far,
        next_stats,
        nxt,
    )
    codes = lax.all_to_all(codes, "cols", 0, 0)
    square = shape(W, W, dtype=bf16)
    near_h, near_l, next_h, next_l, back_h, back_l = call(unpack, (square,) * 6, codes, diagonal_row)

    def step(part, came, nxt):
        w, left, right = call(
            gather_in, (vector, code, code), part, came, nxt, back_h, back_l, next_h, next_l
        )
        came = lax.ppermute(right, "genome", to_right)
        nxt = lax.ppermute(left, "genome", to_left)
        return w, came, nxt, call(inward, vector, w, near_h, near_l)

    came = lax.ppermute(call(outward, code, z, next_h, next_l), "genome", to_right)
    one, came, nxt, part = step(call(inward, vector, z, near_h, near_l), came, z_next)
    two, came, nxt, part = step(part, came, nxt)
    early = call(early_moments, shape(8, 256), z, one, two)
    three, moments = call(
        last_vector, (vector, shape(blocks, 8, 256)), part, came, nxt, back_h, back_l, two, early
    )
    moments = lax.all_to_all(moments, "genome", 0, 0)
    effects, residual = call(combine, (jax.ShapeDtypeStruct(z.shape, f32),) * 2, moments, z, one, two, three)
    return effects.T, residual.T


def solution(mesh):
    return jax.shard_map(
        shards,
        mesh=mesh,
        in_specs=(P("cols", "genome"), P("genome", "cols")),
        out_specs=(P("genome", "cols"), P("genome", "cols")),
        check_vma=False,
    )
```

```python
import functools

import jax
import jax.numpy as jnp
from jax import lax
from jax.experimental import pallas as pl
from jax.experimental.pallas import tpu as pltpu
from jax.sharding import PartitionSpec as P


W = 512
RIDGE = 0.1
FLOOR = 0.02
TILE = 128
SIDE = W // TILE
UPPER = tuple((p, q) for p in range(SIDE) for q in range(p, SIDE))
LOWER = tuple((p, q) for p in range(SIDE) for q in range(p + 1))
NT = len(UPPER)
CODE = 32000.0
HALF = 32768
f32, bf16, i16, i32 = jnp.float32, jnp.bfloat16, jnp.int16, jnp.int32


def dot(a, b):
    return jnp.dot(a, b, preferred_element_type=f32)


def halves(a):
    high = a.astype(bf16)
    return high, (a - high.astype(f32)).astype(bf16)


def call(kernel, outs, *args):
    spec = pl.BlockSpec(memory_space=pltpu.VMEM)
    scalars = [a.dtype == i32 and a.ndim == 1 for a in args]
    return pl.pallas_call(
        kernel,
        out_shape=outs,
        in_specs=[pl.BlockSpec(memory_space=pltpu.SMEM) if s else spec for s in scalars],
        out_specs=jax.tree.map(lambda _: spec, outs, is_leaf=lambda o: not isinstance(o, tuple)),
        compiler_params=pltpu.CompilerParams(vmem_limit_bytes=16 << 20),
    )(*(a if s else pltpu.with_memory_space_constraint(a, pltpu.VMEM) for a, s in zip(args, scalars)))


def shape(*dims, dtype=f32):
    return pltpu.VMEM(dims, dtype)


def tile_of(matrix, p, q):
    return matrix[p * TILE : (p + 1) * TILE, q * TILE : (q + 1) * TILE]


def pack_tiles(gram, tiles, put, peers):
    rows = TILE // peers
    pieces = [tile_of(gram, p, q).reshape(peers, rows, TILE) for p, q in tiles]
    for u in range(len(tiles) // 2):
        pair = jnp.concatenate(pieces[2 * u : 2 * u + 2], axis=1)
        put(2 * rows * u, pair.astype(i32).astype(i16))


def on_diagonal():
    return lax.broadcasted_iota(i32, (TILE, TILE), 0) == lax.broadcasted_iota(i32, (TILE, TILE), 1)


def sums(block, peers):
    ones = jnp.ones((8, block.shape[0]), bf16)
    both = (dot(ones, block)[:1], dot(ones, block * block)[:1])
    stats = [v[:, q * TILE : (q + 1) * TILE] for v in both for q in range(SIDE)]
    stats = jnp.concatenate(stats + [jnp.zeros((8, TILE), f32)], axis=0)
    return jnp.broadcast_to(stats.astype(i32).astype(i16)[None], (peers, 16, TILE))


def own_products(x_ref, out_ref):
    block = x_ref[...]
    near, depth = out_ref.shape[0], out_ref.shape[1] // 2
    peers = 2 * near

    def put(at, value):
        for far in range(2):
            lo = far * depth + at
            out_ref[:, lo : lo + value.shape[1], :] = value[far * near : (far + 1) * near]

    pack_tiles(dot(block.T, block), UPPER, put, peers)
    put(NT * TILE // peers, sums(block, peers))


def next_products(x_ref, next_ref, out_ref):
    block = next_ref[...]
    peers = out_ref.shape[0]

    def put(at, value):
        out_ref[:, at : at + value.shape[1], :] = value

    pack_tiles(dot(x_ref[...].T, block), LOWER, put, peers)
    put(NT * TILE // peers, sums(block, peers))


def fold(me_ref, came_ref, keep_ref, send_ref):
    near, depth = came_ref.shape[0], came_ref.shape[1] // 2
    far = me_ref[0] // near

    def total(side):
        rows = pl.ds(pl.multiple_of(side * depth, depth), depth)
        acc = came_ref[0, rows, :].astype(i32)
        for k in range(1, near):
            acc = acc + came_ref[k, rows, :].astype(i32)
        return acc

    keep_ref[...] = total(far)
    send_ref[...] = (total(1 - far) - HALF).astype(i16)


def correlate(samples, me_ref, keep_ref, far_ref, next_ref, out_ref, diagonal_ref):
    peers = next_ref.shape[0]
    rows = TILE // peers
    own = keep_ref[...] + far_ref[...].astype(i32) + HALF
    nxt = next_ref[0].astype(i32)
    for k in range(1, peers):
        nxt = nxt + next_ref[k].astype(i32)
    own, nxt = own.astype(f32) / samples, nxt.astype(f32) / samples

    def stats(means):
        mean, square = means[:SIDE], means[SIDE : 2 * SIDE]
        variance = square - mean * mean
        return mean, variance, 1.0 / jnp.sqrt(jnp.maximum(variance, FLOOR))

    mean, variance, scale = stats(own[NT * rows :])
    next_mean, _, next_scale = stats(nxt[NT * rows :])
    diagonal_ref[...] = jnp.concatenate([variance * scale * scale, jnp.zeros((8 - SIDE, TILE), f32)], axis=0)
    lane = lax.broadcasted_iota(i32, (rows, TILE), 1)
    row = lax.broadcasted_iota(i32, (rows, TILE), 0) + me_ref[0] * rows

    def at_rows(vector, p):
        return jnp.sum(jnp.where(lane == row, vector[p : p + 1], 0.0), axis=1, keepdims=True)

    row_mean = [at_rows(mean, p) for p in range(SIDE)]
    row_scale = [at_rows(scale, p) * CODE for p in range(SIDE)]

    def code(means, t, p, q, col_mean, col_scale):
        cov = means[t * rows : (t + 1) * rows] - row_mean[p] * col_mean[q : q + 1]
        return jnp.round(cov * row_scale[p] * col_scale[q : q + 1])

    upper = {(p, q): code(own, t, p, q, mean, scale) for t, (p, q) in enumerate(UPPER)}
    lower = {(p, q): code(nxt, t, p, q, next_mean, next_scale) for t, (p, q) in enumerate(LOWER)}
    codes = []
    for p in range(SIDE):
        for q in range(SIDE):
            if p == q:
                codes.append(jnp.where(lane > row, upper[p, q], lower[p, q]))
            else:
                codes.append(upper[p, q] if p < q else lower[p, q])
    codes = jnp.concatenate(codes, axis=0).astype(i32).astype(i16)
    for k in range(peers):
        out_ref[k] = codes


def taper(p, q, shift):
    row = lax.broadcasted_iota(i32, (TILE, TILE), 0) + p * TILE
    col = lax.broadcasted_iota(i32, (TILE, TILE), 1) + q * TILE + shift
    reach = jnp.abs(col - row).astype(f32)
    return jnp.maximum(1.0 - reach / (W + 1), 0.0)


def unpack(codes_ref, diagonal_ref, near_high, near_low, next_high, next_low, back_high, back_low):
    peers = codes_ref.shape[0]
    rows = TILE // peers

    def put(high_ref, low_ref, p, q, value):
        high, low = halves(value)
        high_ref[p * TILE : (p + 1) * TILE, q * TILE : (q + 1) * TILE] = high
        low_ref[p * TILE : (p + 1) * TILE, q * TILE : (q + 1) * TILE] = low

    def put_near(p, q, code):
        value = code * (taper(p, q, 0) * (1.0 / CODE))
        if p == q:
            value = value + value.T
            value = jnp.where(on_diagonal(), diagonal_ref[p : p + 1, :], value)
            put(near_high, near_low, p, q, value)
        else:
            put(near_high, near_low, p, q, value)
            put(near_high, near_low, q, p, value.T)

    def put_next(p, q, code):
        value = code * (taper(p, q, W) * (1.0 / CODE))
        put(next_high, next_low, p, q, value)
        put(back_high, back_low, q, p, value.T)

    strict = lax.broadcasted_iota(i32, (TILE, TILE), 0) < lax.broadcasted_iota(i32, (TILE, TILE), 1)
    zero = jnp.zeros((TILE, TILE), f32)
    for p in range(SIDE):
        for u in range(SIDE // 2):
            lo = 2 * rows * (p * SIDE // 2 + u)
            pair = codes_ref[:, lo : lo + 2 * rows, :].astype(i32).astype(f32)
            for q, code in ((2 * u, pair[:, :rows]), (2 * u + 1, pair[:, rows:])):
                code = code.reshape(TILE, TILE)
                if p <= q:
                    put_near(p, q, jnp.where(strict, code, 0.0) if p == q else code)
                if p >= q:
                    put_next(p, q, code)
                else:
                    put(next_high, next_low, p, q, zero)
                    put(back_high, back_low, q, p, zero)


def product(v, high_ref, low_ref):
    high, low = halves(v)
    return dot(high, high_ref[...]) + dot(low, high_ref[...]) + dot(high, low_ref[...])


def diagonal(rows):
    return lax.broadcasted_iota(i32, (rows, 256), 0) == lax.broadcasted_iota(i32, (rows, 256), 1)


def encode(v, out_ref):
    rows = v.shape[0]
    top = jnp.max(jnp.abs(v), axis=1, keepdims=True)
    power = jnp.ceil(jnp.log2(jnp.maximum(top, 1e-30)) + 0.01)
    code = jnp.round(v * (jnp.exp2(-power) * CODE))
    turned = jnp.sum(jnp.where(diagonal(rows), power, 0.0), axis=0, keepdims=True)
    tail = jnp.broadcast_to(jnp.concatenate([turned, turned], axis=1), (out_ref.shape[0] - rows, v.shape[1]))
    out_ref[...] = jnp.concatenate([code, tail], axis=0).astype(i32).astype(i16)


def decode(code_ref, rows):
    code = code_ref[...].astype(i32).astype(f32)
    power = jnp.sum(jnp.where(diagonal(rows), code[rows : rows + 1, :256], 0.0), axis=1, keepdims=True)
    return code[:rows] * (jnp.exp2(power) * (1.0 / CODE))


def start_code(v_ref, out_ref):
    encode(v_ref[...], out_ref)


def outward(v_ref, high_ref, low_ref, out_ref):
    encode(product(v_ref[...], high_ref, low_ref), out_ref)


def inward(v_ref, high_ref, low_ref, out_ref):
    out_ref[...] = product(v_ref[...], high_ref, low_ref) + RIDGE * v_ref[...]


def gather(part_ref, came_ref, next_ref, high_ref, low_ref):
    rows = part_ref.shape[0]
    return part_ref[...] + decode(came_ref, rows) + product(decode(next_ref, rows), high_ref, low_ref)


def gather_in(part_ref, came_ref, next_ref, back_h, back_l, next_h, next_l, out_ref, left_ref, right_ref):
    w = gather(part_ref, came_ref, next_ref, back_h, back_l)
    out_ref[...] = w
    encode(w, left_ref)
    encode(product(w, next_h, next_l), right_ref)


def along(a, b):
    return jnp.sum(a * b, axis=1, keepdims=True)


def turn(moment):
    return jnp.sum(jnp.where(diagonal(moment.shape[0]), moment, 0.0), axis=0, keepdims=True)


def early_moments(a_ref, b_ref, c_ref, out_ref):
    a, b, c = a_ref[...], b_ref[...], c_ref[...]
    rows = [turn(m) for m in (along(a, a), along(a, b), along(b, b), along(b, c), along(c, c))]
    out_ref[...] = jnp.concatenate(rows + [jnp.zeros((3, 256), f32)], axis=0)


def last_vector(part_ref, came_ref, next_ref, back_h, back_l, c_ref, early_ref, out_ref, moments_ref):
    w = gather(part_ref, came_ref, next_ref, back_h, back_l)
    out_ref[...] = w
    row = lax.broadcasted_iota(i32, early_ref.shape, 0)
    moments = jnp.where(row == 5, turn(along(c_ref[...], w)), early_ref[...])
    for k in range(moments_ref.shape[0]):
        moments_ref[k] = moments


def combine(moments_ref, a_ref, b_ref, c_ref, d_ref, effects_ref, residual_ref):
    total = moments_ref[0]
    for k in range(1, moments_ref.shape[0]):
        total = total + moments_ref[k]
    moment = [total[k : k + 1] / total[:1] for k in range(6)]

    def inner(x, y, power):
        return sum(
            x[i] * y[j] * moment[i + j + power] for i in range(len(x)) for j in range(len(y))
        )

    one = jnp.ones_like(moment[0])
    residual, direction, effects = [one], [one], []
    norm_now = inner(residual, residual, 0)
    for step in range(3):
        step_size = norm_now / inner(direction, direction, 1)
        effects = [
            (effects[k] if k < len(effects) else 0.0) + step_size * direction[k] for k in range(len(direction))
        ]
        image = [0.0] + direction
        residual = [
            (residual[k] if k < len(residual) else 0.0) - step_size * image[k] for k in range(len(image))
        ]
        if step < 2:
            norm_next = inner(residual, residual, 0)
            ratio = norm_next / norm_now
            direction = [
                residual[k] + (ratio * direction[k] if k < len(direction) else 0.0) for k in range(len(residual))
            ]
            norm_now = norm_next
    rows = effects + residual
    table = jnp.concatenate(rows + [jnp.zeros((TILE - len(rows), total.shape[1]), f32)], axis=0).T
    table = table[: a_ref.shape[0]]
    col = [table[:, k : k + 1] for k in range(len(rows))]
    a, b, c, d = a_ref[...], b_ref[...], c_ref[...], d_ref[...]
    effects_ref[...] = col[0] * a + col[1] * b + col[2] * c
    residual_ref[...] = col[3] * a + col[4] * b + col[5] * c + col[6] * d


def shards(genotypes, z_scores):
    local_samples, _ = genotypes.shape
    blocks = lax.axis_size("genome")
    peers = lax.axis_size("cols")
    samples = local_samples * peers
    to_left = [(k + 1, k) for k in range(blocks - 1)]
    to_right = [(k, k + 1) for k in range(blocks - 1)]
    rows = TILE // peers

    near = peers // 2
    depth = NT * rows + 16
    cols = range(peers)
    sides = [list(cols[:near]), list(cols[near:])]

    dosage = genotypes.astype(bf16)
    next_dosage = lax.ppermute(dosage, "genome", to_left)
    own = call(own_products, shape(near, 2 * depth, TILE, dtype=i16), dosage)
    own = lax.all_to_all(own, "cols", 0, 0, axis_index_groups=sides)
    me = lax.axis_index("cols").astype(i32).reshape(1)
    keep, far = call(fold, (shape(depth, TILE, dtype=i32), shape(depth, TILE, dtype=i16)), me, own)
    z = z_scores.T
    vector = shape(*z.shape)
    code = shape(z.shape[0] // 16 * 16 + 16, z.shape[1], dtype=i16)
    z_code = call(start_code, code, z)
    far, next_dosage = lax.optimization_barrier((far, next_dosage))
    far = lax.ppermute(far, "cols", [(k, (k + near) % peers) for k in cols])
    nxt = call(next_products, shape(peers, depth, TILE, dtype=i16), dosage, next_dosage)
    z_code, nxt = lax.optimization_barrier((z_code, nxt))
    nxt = lax.all_to_all(nxt, "cols", 0, 0)
    z_next = lax.ppermute(z_code, "genome", to_left)
    codes, diagonal_row = call(
        functools.partial(correlate, samples),
        (shape(peers, SIDE * SIDE * rows, TILE, dtype=i16), shape(8, TILE)),
        me,
        keep,
        far,
        nxt,
    )
    codes = lax.all_to_all(codes, "cols", 0, 0)
    square = shape(W, W, dtype=bf16)
    near_h, near_l, next_h, next_l, back_h, back_l = call(unpack, (square,) * 6, codes, diagonal_row)

    def step(part, came, nxt):
        w, left, right = call(
            gather_in, (vector, code, code), part, came, nxt, back_h, back_l, next_h, next_l
        )
        came = lax.ppermute(right, "genome", to_right)
        nxt = lax.ppermute(left, "genome", to_left)
        return w, came, nxt, call(inward, vector, w, near_h, near_l)

    came = lax.ppermute(call(outward, code, z, next_h, next_l), "genome", to_right)
    one, came, nxt, part = step(call(inward, vector, z, near_h, near_l), came, z_next)
    two, came, nxt, part = step(part, came, nxt)
    early = call(early_moments, shape(8, 256), z, one, two)
    three, moments = call(
        last_vector, (vector, shape(blocks, 8, 256)), part, came, nxt, back_h, back_l, two, early
    )
    moments = lax.all_to_all(moments, "genome", 0, 0)
    effects, residual = call(combine, (jax.ShapeDtypeStruct(z.shape, f32),) * 2, moments, z, one, two, three)
    return effects.T, residual.T


def solution(mesh):
    return jax.shard_map(
        shards,
        mesh=mesh,
        in_specs=(P("cols", "genome"), P("genome", "cols")),
        out_specs=(P("genome", "cols"), P("genome", "cols")),
        check_vma=False,
    )
```

```python
import functools

import jax
import jax.numpy as jnp
from jax import lax
from jax.experimental import pallas as pl
from jax.experimental.pallas import tpu as pltpu
from jax.sharding import PartitionSpec as P


W = 512
RIDGE = 0.1
FLOOR = 0.02
TILE = 128
SIDE = W // TILE
UPPER = tuple((p, q) for p in range(SIDE) for q in range(p, SIDE))
LOWER = tuple((p, q) for p in range(SIDE) for q in range(p + 1))
NT = len(UPPER)
CODE = 32000.0
HALF = 32768
f32, bf16, i16, i32 = jnp.float32, jnp.bfloat16, jnp.int16, jnp.int32


def dot(a, b):
    return jnp.dot(a, b, preferred_element_type=f32)


def halves(a):
    high = a.astype(bf16)
    return high, (a - high.astype(f32)).astype(bf16)


def call(kernel, outs, *args, far=(), scratch=()):
    spec = pl.BlockSpec(memory_space=pltpu.VMEM)
    return pl.pallas_call(
        kernel,
        out_shape=outs,
        in_specs=[pl.BlockSpec(memory_space=pl.ANY) if k in far else spec for k in range(len(args))],
        scratch_shapes=scratch,
        out_specs=jax.tree.map(lambda _: spec, outs, is_leaf=lambda o: not isinstance(o, tuple)),
        compiler_params=pltpu.CompilerParams(vmem_limit_bytes=16 << 20),
    )(*(a if k in far else pltpu.with_memory_space_constraint(a, pltpu.VMEM) for k, a in enumerate(args)))


def shape(*dims, dtype=f32):
    return pltpu.VMEM(dims, dtype)


def tile_of(matrix, p, q):
    return matrix[p * TILE : (p + 1) * TILE, q * TILE : (q + 1) * TILE]


def pack_tiles(gram, tiles, put, peers):
    rows = TILE // peers
    pieces = [tile_of(gram, p, q).reshape(peers, rows, TILE) for p, q in tiles]
    for u in range(len(tiles) // 2):
        pair = jnp.concatenate(pieces[2 * u : 2 * u + 2], axis=1)
        put(2 * rows * u, pair.astype(i32).astype(i16))


def on_diagonal():
    return lax.broadcasted_iota(i32, (TILE, TILE), 0) == lax.broadcasted_iota(i32, (TILE, TILE), 1)


def sums(block, peers):
    high = 0.0, 0.0
    step = 16
    for lo in range(0, block.shape[0], 60 * step):
        near = square = None
        for at in range(lo, min(lo + 60 * step, block.shape[0]), step):
            x = block[at : at + step]
            near, square = (x, x * x) if near is None else (near + x, square + x * x)
        high = high[0] + near.astype(f32), high[1] + square.astype(f32)
    both = [jnp.sum(v, axis=0, keepdims=True) for v in high]
    stats = [v[:, q * TILE : (q + 1) * TILE] for v in both for q in range(SIDE)]
    stats = jnp.concatenate(stats + [jnp.zeros((8, TILE), f32)], axis=0)
    return jnp.broadcast_to(stats.astype(i32).astype(i16)[None], (peers, 16, TILE))


def own_products(x_ref, out_ref):
    block = x_ref[...]
    near, depth = out_ref.shape[0], out_ref.shape[1] // 2
    peers = 2 * near

    def put(at, value):
        for far in range(2):
            lo = far * depth + at
            out_ref[:, lo : lo + value.shape[1], :] = value[far * near : (far + 1) * near]

    pack_tiles(dot(block.T, block), UPPER, put, peers)
    put(NT * TILE // peers, sums(block, peers))


def next_products(x_ref, next_ref, out_ref, block_ref, sem):
    peers = out_ref.shape[0]
    parts = sem.shape[0]
    length = block_ref.shape[0] // parts
    spans = [pl.ds(k * length, length) for k in range(parts)]
    copies = [
        pltpu.make_async_copy(next_ref.at[span], block_ref.at[span], sem.at[k]) for k, span in enumerate(spans)
    ]
    for copy in copies:
        copy.start()
    gram = None
    for copy, span in zip(copies, spans):
        turned = x_ref[span].T
        copy.wait()
        more = dot(turned, block_ref[span])
        gram = more if gram is None else gram + more

    def put(at, value):
        out_ref[:, at : at + value.shape[1], :] = value

    pack_tiles(gram, LOWER, put, peers)
    put(NT * TILE // peers, sums(block_ref[...], peers))


def fold(came_ref, keep_ref, send_ref):
    near, depth = came_ref.shape[0], came_ref.shape[1] // 2
    far = lax.axis_index("cols") // near

    def total(side):
        rows = pl.ds(pl.multiple_of(side * depth, depth), depth)
        acc = came_ref[0, rows, :].astype(i32)
        for k in range(1, near):
            acc = acc + came_ref[k, rows, :].astype(i32)
        return acc

    keep_ref[...] = total(far)
    send_ref[...] = (total(1 - far) - HALF).astype(i16)


def correlate(samples, keep_ref, far_ref, next_ref, out_ref, diagonal_ref):
    peers = next_ref.shape[0]
    rows = TILE // peers
    own = keep_ref[...] + far_ref[...].astype(i32) + HALF
    nxt = next_ref[0].astype(i32)
    for k in range(1, peers):
        nxt = nxt + next_ref[k].astype(i32)
    own, nxt = own.astype(f32) / samples, nxt.astype(f32) / samples

    def stats(means):
        mean, square = means[:SIDE], means[SIDE : 2 * SIDE]
        variance = square - mean * mean
        return mean, variance, 1.0 / jnp.sqrt(jnp.maximum(variance, FLOOR))

    mean, variance, scale = stats(own[NT * rows :])
    next_mean, _, next_scale = stats(nxt[NT * rows :])
    diagonal_ref[...] = jnp.concatenate([variance * scale * scale, jnp.zeros((8 - SIDE, TILE), f32)], axis=0)
    lane = lax.broadcasted_iota(i32, (rows, TILE), 1)
    row = lax.broadcasted_iota(i32, (rows, TILE), 0) + lax.axis_index("cols") * rows

    def at_rows(vector, p):
        return jnp.sum(jnp.where(lane == row, vector[p : p + 1], 0.0), axis=1, keepdims=True)

    row_mean = [at_rows(mean, p) for p in range(SIDE)]
    row_scale = [at_rows(scale, p) * CODE for p in range(SIDE)]

    def code(means, t, p, q, col_mean, col_scale):
        cov = means[t * rows : (t + 1) * rows] - row_mean[p] * col_mean[q : q + 1]
        return jnp.round(cov * row_scale[p] * col_scale[q : q + 1])

    upper = {(p, q): code(own, t, p, q, mean, scale) for t, (p, q) in enumerate(UPPER)}
    lower = {(p, q): code(nxt, t, p, q, next_mean, next_scale) for t, (p, q) in enumerate(LOWER)}
    codes = []
    for p in range(SIDE):
        for q in range(SIDE):
            if p == q:
                codes.append(jnp.where(lane > row, upper[p, q], lower[p, q]))
            else:
                codes.append(upper[p, q] if p < q else lower[p, q])
    codes = jnp.concatenate(codes, axis=0).astype(i32).astype(i16)
    for k in range(peers):
        out_ref[k] = codes


def taper(p, q, shift):
    row = lax.broadcasted_iota(i32, (TILE, TILE), 0) + p * TILE
    col = lax.broadcasted_iota(i32, (TILE, TILE), 1) + q * TILE + shift
    reach = jnp.abs(col - row).astype(f32)
    return jnp.maximum(1.0 - reach / (W + 1), 0.0)


def unpack(codes_ref, diagonal_ref, near_high, near_low, next_high, next_low, back_high, back_low):
    peers = codes_ref.shape[0]
    rows = TILE // peers

    def put(high_ref, low_ref, p, q, value):
        high, low = halves(value)
        high_ref[p * TILE : (p + 1) * TILE, q * TILE : (q + 1) * TILE] = high
        low_ref[p * TILE : (p + 1) * TILE, q * TILE : (q + 1) * TILE] = low

    def put_near(p, q, code):
        value = code * (taper(p, q, 0) * (1.0 / CODE))
        if p == q:
            value = value + value.T
            value = jnp.where(on_diagonal(), diagonal_ref[p : p + 1, :], value)
            put(near_high, near_low, p, q, value)
        else:
            put(near_high, near_low, p, q, value)
            put(near_high, near_low, q, p, value.T)

    def put_next(p, q, code):
        value = code * (taper(p, q, W) * (1.0 / CODE))
        put(next_high, next_low, p, q, value)
        put(back_high, back_low, q, p, value.T)

    strict = lax.broadcasted_iota(i32, (TILE, TILE), 0) < lax.broadcasted_iota(i32, (TILE, TILE), 1)
    zero = jnp.zeros((TILE, TILE), f32)
    for p in range(SIDE):
        for u in range(SIDE // 2):
            lo = 2 * rows * (p * SIDE // 2 + u)
            pair = codes_ref[:, lo : lo + 2 * rows, :].astype(i32).astype(f32)
            for q, code in ((2 * u, pair[:, :rows]), (2 * u + 1, pair[:, rows:])):
                code = code.reshape(TILE, TILE)
                if p <= q:
                    put_near(p, q, jnp.where(strict, code, 0.0) if p == q else code)
                if p >= q:
                    put_next(p, q, code)
                else:
                    put(next_high, next_low, p, q, zero)
                    put(back_high, back_low, q, p, zero)


def product(v, high_ref, low_ref):
    high, low = halves(v)
    return dot(high, high_ref[...]) + dot(low, high_ref[...]) + dot(high, low_ref[...])


def diagonal(rows):
    return lax.broadcasted_iota(i32, (rows, 256), 0) == lax.broadcasted_iota(i32, (rows, 256), 1)


def encode(v, out_ref):
    rows = v.shape[0]
    top = jnp.max(jnp.abs(v), axis=1, keepdims=True)
    power = jnp.ceil(jnp.log2(jnp.maximum(top, 1e-30)) + 0.01)
    code = jnp.round(v * (jnp.exp2(-power) * CODE))
    turned = jnp.sum(jnp.where(diagonal(rows), power, 0.0), axis=0, keepdims=True)
    tail = jnp.broadcast_to(jnp.concatenate([turned, turned], axis=1), (out_ref.shape[0] - rows, v.shape[1]))
    out_ref[...] = jnp.concatenate([code, tail], axis=0).astype(i32).astype(i16)


def decode(code, rows):
    code = code.astype(i32).astype(f32)
    power = jnp.sum(jnp.where(diagonal(rows), code[rows : rows + 1, :256], 0.0), axis=1, keepdims=True)
    return code[:rows] * (jnp.exp2(power) * (1.0 / CODE))


def start_code(v_ref, out_ref):
    encode(v_ref[...], out_ref)


def outward(v_ref, high_ref, low_ref, out_ref):
    encode(product(v_ref[...], high_ref, low_ref), out_ref)


def inward(v_ref, high_ref, low_ref, out_ref):
    out_ref[...] = product(v_ref[...], high_ref, low_ref) + RIDGE * v_ref[...]


def gather(part_ref, came, nxt, back_h, back_l):
    rows = part_ref.shape[0]
    return part_ref[...] + decode(came, rows) + product(decode(nxt, rows), back_h, back_l)


def first_gather(part_ref, came_ref, next_ref, back_h, back_l, next_h, next_l, out_ref, across_ref, inside_ref):
    w = gather(part_ref, came_ref[...], next_ref[...], back_h, back_l)
    hand_on(w, next_h, next_l, out_ref, across_ref, inside_ref)


def next_gather(part_ref, across_in, inside_in, back_h, back_l, next_h, next_l, out_ref, across_ref, inside_ref):
    w = gather(part_ref, *arrived(across_in, inside_in), back_h, back_l)
    hand_on(w, next_h, next_l, out_ref, across_ref, inside_ref)


def odd():
    return lax.rem(lax.axis_index("genome"), 2)


def hand_on(w, next_h, next_l, out_ref, across_ref, inside_ref):
    out_ref[...] = w

    @pl.when(odd() == 0)
    def _():
        encode(w, across_ref)
        encode(product(w, next_h, next_l), inside_ref)

    @pl.when(odd() == 1)
    def _():
        encode(product(w, next_h, next_l), across_ref)
        encode(w, inside_ref)


def arrived(across_in, inside_in):
    even = odd() == 0
    across, inside = across_in[...].astype(i32), inside_in[...].astype(i32)
    return jnp.where(even, across, inside), jnp.where(even, inside, across)


def along(a, b):
    return jnp.sum(a * b, axis=1, keepdims=True)


def turn(moment):
    return jnp.sum(jnp.where(diagonal(moment.shape[0]), moment, 0.0), axis=0, keepdims=True)


def early_moments(a_ref, b_ref, c_ref, out_ref):
    a, b, c = a_ref[...], b_ref[...], c_ref[...]
    rows = [turn(m) for m in (along(a, a), along(a, b), along(b, b), along(b, c), along(c, c))]
    out_ref[...] = jnp.concatenate(rows + [jnp.zeros((3, 256), f32)], axis=0)


def last_vector(part_ref, across_in, inside_in, back_h, back_l, c_ref, early_ref, out_ref, moments_ref):
    w = gather(part_ref, *arrived(across_in, inside_in), back_h, back_l)
    out_ref[...] = w
    row = lax.broadcasted_iota(i32, early_ref.shape, 0)
    moments = jnp.where(row == 5, turn(along(c_ref[...], w)), early_ref[...])
    for k in range(moments_ref.shape[0]):
        moments_ref[k] = moments


def combine(moments_ref, a_ref, b_ref, c_ref, d_ref, effects_ref, residual_ref):
    total = moments_ref[0]
    for k in range(1, moments_ref.shape[0]):
        total = total + moments_ref[k]
    moment = [total[k : k + 1] / total[:1] for k in range(6)]

    def inner(x, y, power):
        return sum(
            x[i] * y[j] * moment[i + j + power] for i in range(len(x)) for j in range(len(y))
        )

    one = jnp.ones_like(moment[0])
    residual, direction, effects = [one], [one], []
    norm_now = inner(residual, residual, 0)
    for step in range(3):
        step_size = norm_now / inner(direction, direction, 1)
        effects = [
            (effects[k] if k < len(effects) else 0.0) + step_size * direction[k] for k in range(len(direction))
        ]
        image = [0.0] + direction
        residual = [
            (residual[k] if k < len(residual) else 0.0) - step_size * image[k] for k in range(len(image))
        ]
        if step < 2:
            norm_next = inner(residual, residual, 0)
            ratio = norm_next / norm_now
            direction = [
                residual[k] + (ratio * direction[k] if k < len(direction) else 0.0) for k in range(len(residual))
            ]
            norm_now = norm_next
    rows = effects + residual
    table = jnp.concatenate(rows + [jnp.zeros((TILE - len(rows), total.shape[1]), f32)], axis=0).T
    table = table[: a_ref.shape[0]]
    col = [table[:, k : k + 1] for k in range(len(rows))]
    a, b, c, d = a_ref[...], b_ref[...], c_ref[...], d_ref[...]
    effects_ref[...] = col[0] * a + col[1] * b + col[2] * c
    residual_ref[...] = col[3] * a + col[4] * b + col[5] * c + col[6] * d


def shards(genotypes, z_scores):
    local_samples, _ = genotypes.shape
    blocks = lax.axis_size("genome")
    peers = lax.axis_size("cols")
    samples = local_samples * peers
    to_left = [(k + 1, k) for k in range(blocks - 1)]
    to_right = [(k, k + 1) for k in range(blocks - 1)]
    rows = TILE // peers

    near = peers // 2
    depth = NT * rows + 16
    cols = range(peers)
    sides = [list(cols[:near]), list(cols[near:])]

    dosage = genotypes.astype(bf16)
    next_dosage = lax.ppermute(dosage, "genome", to_left)
    own = call(own_products, shape(near, 2 * depth, TILE, dtype=i16), dosage)
    own = lax.all_to_all(own, "cols", 0, 0, axis_index_groups=sides)
    keep, far = call(fold, (shape(depth, TILE, dtype=i32), shape(depth, TILE, dtype=i16)), own)
    z = z_scores.T
    vector = shape(*z.shape)
    code = shape(z.shape[0] // 16 * 16 + 16, z.shape[1], dtype=i16)
    z_code = call(start_code, code, z)
    far, next_dosage = lax.optimization_barrier((far, next_dosage))
    far = lax.ppermute(far, "cols", [(k, (k + near) % peers) for k in cols])
    nxt = call(
        next_products,
        shape(peers, depth, TILE, dtype=i16),
        dosage,
        next_dosage,
        far=(1,),
        scratch=(pltpu.VMEM(dosage.shape, bf16), pltpu.SemaphoreType.DMA((5,))),
    )
    z_code, nxt = lax.optimization_barrier((z_code, nxt))
    nxt = lax.all_to_all(nxt, "cols", 0, 0)
    z_next = lax.ppermute(z_code, "genome", to_left)
    codes, diagonal_row = call(
        functools.partial(correlate, samples),
        (shape(peers, SIDE * SIDE * rows, TILE, dtype=i16), shape(8, TILE)),
        keep,
        far,
        nxt,
    )
    codes = lax.all_to_all(codes, "cols", 0, 0)
    square = shape(W, W, dtype=bf16)
    near_h, near_l, next_h, next_l, back_h, back_l = call(unpack, (square,) * 6, codes, diagonal_row)

    inside = [(k, k ^ 1) for k in range(blocks)]
    across = [(k, ((k + 1) ^ 1) - 1) for k in range(1, blocks - 1)]

    def step(kernel, part, *came):
        w, out, inn = call(
            kernel, (vector, code, code), part, *came, back_h, back_l, next_h, next_l
        )
        out = lax.ppermute(out, "genome", across)
        inn = lax.ppermute(inn, "genome", inside)
        return w, call(inward, vector, w, near_h, near_l), out, inn

    came = lax.ppermute(call(outward, code, z, next_h, next_l), "genome", to_right)
    one, *rest = step(first_gather, call(inward, vector, z, near_h, near_l), came, z_next)
    two, part, out, inn = step(next_gather, *rest)
    early = call(early_moments, shape(8, 256), z, one, two)
    three, moments = call(
        last_vector, (vector, shape(blocks, 8, 256)), part, out, inn, back_h, back_l, two, early
    )
    moments = lax.all_to_all(moments, "genome", 0, 0)
    effects, residual = call(combine, (jax.ShapeDtypeStruct(z.shape, f32),) * 2, moments, z, one, two, three)
    return effects.T, residual.T


def solution(mesh):
    return jax.shard_map(
        shards,
        mesh=mesh,
        in_specs=(P("cols", "genome"), P("genome", "cols")),
        out_specs=(P("genome", "cols"), P("genome", "cols")),
        check_vma=False,
    )
```

```python
import functools

import jax
import jax.numpy as jnp
from jax import lax
from jax.experimental import pallas as pl
from jax.experimental.pallas import tpu as pltpu
from jax.sharding import PartitionSpec as P


W = 512
RIDGE = 0.1
FLOOR = 0.02
TILE = 128
SIDE = W // TILE
UPPER = tuple((p, q) for p in range(SIDE) for q in range(p, SIDE))
LOWER = tuple((p, q) for q in range(SIDE) for p in range(q, SIDE))
HEAD = tuple(t for t in LOWER if t[1] < SIDE // 2)
TAIL = tuple(t for t in LOWER if t[1] >= SIDE // 2)
NT = len(UPPER)
CODE = 32000.0
HALF = 32768
f32, bf16, i16, i32 = jnp.float32, jnp.bfloat16, jnp.int16, jnp.int32


def dot(a, b):
    return jnp.dot(a, b, preferred_element_type=f32)


def halves(a):
    high = a.astype(bf16)
    return high, (a - high.astype(f32)).astype(bf16)


def call(kernel, outs, *args):
    spec = pl.BlockSpec(memory_space=pltpu.VMEM)
    return pl.pallas_call(
        kernel,
        out_shape=outs,
        in_specs=[spec] * len(args),
        out_specs=jax.tree.map(lambda _: spec, outs, is_leaf=lambda o: not isinstance(o, tuple)),
        compiler_params=pltpu.CompilerParams(vmem_limit_bytes=16 << 20),
    )(*(pltpu.with_memory_space_constraint(a, pltpu.VMEM) for a in args))


def shape(*dims, dtype=f32):
    return pltpu.VMEM(dims, dtype)


def tile_of(matrix, p, q):
    return matrix[p * TILE : (p + 1) * TILE, q * TILE : (q + 1) * TILE]


def pack_tiles(tiles, block, peers, put):
    rows = TILE // peers
    pieces = [tile.reshape(peers, rows, TILE) for tile in tiles] + sums(block, peers, rows)
    for u in range(len(pieces) // 2):
        pair = jnp.concatenate(pieces[2 * u : 2 * u + 2], axis=1)
        put(2 * rows * u, pair.astype(i32).astype(i16))


def on_diagonal():
    return lax.broadcasted_iota(i32, (TILE, TILE), 0) == lax.broadcasted_iota(i32, (TILE, TILE), 1)


def sums(block, peers, rows):
    high = 0.0, 0.0
    step = 16
    for lo in range(0, block.shape[0], 60 * step):
        near = square = None
        for at in range(lo, min(lo + 60 * step, block.shape[0]), step):
            x = block[at : at + step]
            near, square = (x, x * x) if near is None else (near + x, square + x * x)
        high = high[0] + near.astype(f32), high[1] + square.astype(f32)
    both = [jnp.sum(v, axis=0, keepdims=True) for v in high]
    stats = [v[:, at : at + TILE] for v in both for at in range(0, block.shape[1], TILE)]
    if len(stats) < rows:
        stats.append(jnp.zeros((rows - len(stats), TILE), f32))
    stats = jnp.broadcast_to(jnp.concatenate(stats, axis=0)[None], (peers, rows, TILE))
    return [stats, jnp.zeros_like(stats)] if block.shape[1] == W else [stats]


def own_products(first_ref, second_ref, out_ref):
    block = jnp.concatenate([first_ref[...], second_ref[...]], axis=1)
    near, depth = out_ref.shape[0], out_ref.shape[1] // 2
    peers = 2 * near

    def put(at, value):
        for far in range(2):
            lo = far * depth + at
            out_ref[:, lo : lo + value.shape[1], :] = value[far * near : (far + 1) * near]

    gram = dot(block.T, block)
    pack_tiles([tile_of(gram, p, q) for p, q in UPPER], block, peers, put)


def head_products(first_ref, second_ref, next_ref, out_ref):
    block = next_ref[...]
    grams = dot(first_ref[...].T, block), dot(second_ref[...].T, block)

    def put(at, value):
        out_ref[:, at : at + value.shape[1], :] = value

    half = SIDE // 2
    pack_tiles([tile_of(grams[p // half], p % half, q) for p, q in HEAD], block, out_ref.shape[0], put)


def tail_products(second_ref, next_ref, head_ref, out_ref):
    block = next_ref[...]
    gram = dot(second_ref[...].T, block)
    done = head_ref.shape[1]
    out_ref[:, :done, :] = head_ref[...]

    def put(at, value):
        out_ref[:, done + at : done + at + value.shape[1], :] = value

    half = SIDE // 2
    pack_tiles([tile_of(gram, p - half, q - half) for p, q in TAIL], block, out_ref.shape[0], put)


def fold(came_ref, keep_ref, send_ref):
    near, depth = came_ref.shape[0], came_ref.shape[1] // 2
    far = lax.axis_index("cols") // near

    def total(side):
        rows = pl.ds(pl.multiple_of(side * depth, depth), depth)
        acc = came_ref[0, rows, :].astype(i32)
        for k in range(1, near):
            acc = acc + came_ref[k, rows, :].astype(i32)
        return acc

    keep_ref[...] = total(far)
    send_ref[...] = (total(1 - far) - HALF).astype(i16)


def correlate(samples, keep_ref, far_ref, next_ref, out_ref, diagonal_ref):
    peers = next_ref.shape[0]
    rows = TILE // peers
    own = keep_ref[...] + far_ref[...].astype(i32) + HALF
    nxt = next_ref[0].astype(i32)
    for k in range(1, peers):
        nxt = nxt + next_ref[k].astype(i32)
    own, nxt = own.astype(f32) / samples, nxt.astype(f32) / samples

    def stats(means):
        mean, square = means[:SIDE], means[SIDE : 2 * SIDE]
        variance = square - mean * mean
        return mean, variance, 1.0 / jnp.sqrt(jnp.maximum(variance, FLOOR))

    mean, variance, scale = stats(own[NT * rows :])
    slot = {tile: t for t, tile in enumerate(HEAD + ("head",) + TAIL + ("tail",))}
    half = SIDE // 2
    parts = [nxt[slot[name] * rows : slot[name] * rows + SIDE] for name in ("head", "tail")]
    next_mean, _, next_scale = stats(jnp.concatenate([v[k : k + half] for k in (0, half) for v in parts], axis=0))
    diagonal_ref[...] = jnp.concatenate([variance * scale * scale, jnp.zeros((8 - SIDE, TILE), f32)], axis=0)
    lane = lax.broadcasted_iota(i32, (rows, TILE), 1)
    row = lax.broadcasted_iota(i32, (rows, TILE), 0) + lax.axis_index("cols") * rows

    def at_rows(vector, p):
        return jnp.sum(jnp.where(lane == row, vector[p : p + 1], 0.0), axis=1, keepdims=True)

    row_mean = [at_rows(mean, p) for p in range(SIDE)]
    row_scale = [at_rows(scale, p) * CODE for p in range(SIDE)]

    def code(means, t, p, q, col_mean, col_scale):
        cov = means[t * rows : (t + 1) * rows] - row_mean[p] * col_mean[q : q + 1]
        return jnp.round(cov * row_scale[p] * col_scale[q : q + 1])

    upper = {(p, q): code(own, t, p, q, mean, scale) for t, (p, q) in enumerate(UPPER)}
    lower = {(p, q): code(nxt, slot[p, q], p, q, next_mean, next_scale) for p, q in LOWER}
    codes = []
    for p in range(SIDE):
        for q in range(SIDE):
            if p == q:
                codes.append(jnp.where(lane > row, upper[p, q], lower[p, q]))
            else:
                codes.append(upper[p, q] if p < q else lower[p, q])
    codes = jnp.concatenate(codes, axis=0).astype(i32).astype(i16)
    for k in range(peers):
        out_ref[k] = codes


def taper(p, q, shift):
    row = lax.broadcasted_iota(i32, (TILE, TILE), 0) + p * TILE
    col = lax.broadcasted_iota(i32, (TILE, TILE), 1) + q * TILE + shift
    reach = jnp.abs(col - row).astype(f32)
    return jnp.maximum(1.0 - reach / (W + 1), 0.0)


def unpack(codes_ref, diagonal_ref, near_high, near_low, next_high, next_low, back_high, back_low):
    peers = codes_ref.shape[0]
    rows = TILE // peers

    def put(high_ref, low_ref, p, q, value):
        high, low = halves(value)
        high_ref[p * TILE : (p + 1) * TILE, q * TILE : (q + 1) * TILE] = high
        low_ref[p * TILE : (p + 1) * TILE, q * TILE : (q + 1) * TILE] = low

    def put_near(p, q, code):
        value = code * (taper(p, q, 0) * (1.0 / CODE))
        if p == q:
            value = value + value.T
            value = jnp.where(on_diagonal(), diagonal_ref[p : p + 1, :], value)
            put(near_high, near_low, p, q, value)
        else:
            put(near_high, near_low, p, q, value)
            put(near_high, near_low, q, p, value.T)

    def put_next(p, q, code):
        value = code * (taper(p, q, W) * (1.0 / CODE))
        put(next_high, next_low, p, q, value)
        put(back_high, back_low, q, p, value.T)

    strict = lax.broadcasted_iota(i32, (TILE, TILE), 0) < lax.broadcasted_iota(i32, (TILE, TILE), 1)
    zero = jnp.zeros((TILE, TILE), f32)
    for p in range(SIDE):
        for u in range(SIDE // 2):
            lo = 2 * rows * (p * SIDE // 2 + u)
            pair = codes_ref[:, lo : lo + 2 * rows, :].astype(i32).astype(f32)
            for q, code in ((2 * u, pair[:, :rows]), (2 * u + 1, pair[:, rows:])):
                code = code.reshape(TILE, TILE)
                if p <= q:
                    put_near(p, q, jnp.where(strict, code, 0.0) if p == q else code)
                if p >= q:
                    put_next(p, q, code)
                else:
                    put(next_high, next_low, p, q, zero)
                    put(back_high, back_low, q, p, zero)


def product(v, high_ref, low_ref):
    high, low = halves(v)
    return dot(high, high_ref[...]) + dot(low, high_ref[...]) + dot(high, low_ref[...])


def diagonal(rows):
    return lax.broadcasted_iota(i32, (rows, 256), 0) == lax.broadcasted_iota(i32, (rows, 256), 1)


def encode(v, out_ref):
    rows = v.shape[0]
    top = jnp.max(jnp.abs(v), axis=1, keepdims=True)
    power = jnp.ceil(jnp.log2(jnp.maximum(top, 1e-30)) + 0.01)
    code = jnp.round(v * (jnp.exp2(-power) * CODE))
    turned = jnp.sum(jnp.where(diagonal(rows), power, 0.0), axis=0, keepdims=True)
    tail = jnp.broadcast_to(jnp.concatenate([turned, turned], axis=1), (out_ref.shape[0] - rows, v.shape[1]))
    out_ref[...] = jnp.concatenate([code, tail], axis=0).astype(i32).astype(i16)


def decode(code, rows):
    code = code.astype(i32).astype(f32)
    power = jnp.sum(jnp.where(diagonal(rows), code[rows : rows + 1, :256], 0.0), axis=1, keepdims=True)
    return code[:rows] * (jnp.exp2(power) * (1.0 / CODE))


def start_code(v_ref, out_ref):
    encode(v_ref[...], out_ref)


def outward(v_ref, high_ref, low_ref, out_ref):
    encode(product(v_ref[...], high_ref, low_ref), out_ref)


def inward(v_ref, high_ref, low_ref, out_ref):
    out_ref[...] = product(v_ref[...], high_ref, low_ref) + RIDGE * v_ref[...]


def gather(part_ref, came, nxt, back_h, back_l):
    rows = part_ref.shape[0]
    return part_ref[...] + decode(came, rows) + product(decode(nxt, rows), back_h, back_l)


def first_gather(part_ref, came_ref, next_ref, back_h, back_l, next_h, next_l, out_ref, across_ref, inside_ref):
    w = gather(part_ref, came_ref[...], next_ref[...], back_h, back_l)
    hand_on(w, next_h, next_l, out_ref, across_ref, inside_ref)


def next_gather(part_ref, across_in, inside_in, back_h, back_l, next_h, next_l, out_ref, across_ref, inside_ref):
    w = gather(part_ref, *arrived(across_in, inside_in), back_h, back_l)
    hand_on(w, next_h, next_l, out_ref, across_ref, inside_ref)


def odd():
    return lax.rem(lax.axis_index("genome"), 2)


def hand_on(w, next_h, next_l, out_ref, across_ref, inside_ref):
    out_ref[...] = w

    @pl.when(odd() == 0)
    def _():
        encode(w, across_ref)
        encode(product(w, next_h, next_l), inside_ref)

    @pl.when(odd() == 1)
    def _():
        encode(product(w, next_h, next_l), across_ref)
        encode(w, inside_ref)


def arrived(across_in, inside_in):
    even = odd() == 0
    across, inside = across_in[...].astype(i32), inside_in[...].astype(i32)
    return jnp.where(even, across, inside), jnp.where(even, inside, across)


def along(a, b):
    return jnp.sum(a * b, axis=1, keepdims=True)


def turn(moment):
    return jnp.sum(jnp.where(diagonal(moment.shape[0]), moment, 0.0), axis=0, keepdims=True)


def early_moments(a_ref, b_ref, c_ref, out_ref):
    a, b, c = a_ref[...], b_ref[...], c_ref[...]
    rows = [turn(m) for m in (along(a, a), along(a, b), along(b, b), along(b, c), along(c, c))]
    out_ref[...] = jnp.concatenate(rows + [jnp.zeros((3, 256), f32)], axis=0)


def last_vector(part_ref, across_in, inside_in, back_h, back_l, c_ref, early_ref, out_ref, moments_ref):
    w = gather(part_ref, *arrived(across_in, inside_in), back_h, back_l)
    out_ref[...] = w
    row = lax.broadcasted_iota(i32, early_ref.shape, 0)
    moments = jnp.where(row == 5, turn(along(c_ref[...], w)), early_ref[...])
    for k in range(moments_ref.shape[0]):
        moments_ref[k] = moments


def combine(moments_ref, a_ref, b_ref, c_ref, d_ref, effects_ref, residual_ref):
    total = moments_ref[0]
    for k in range(1, moments_ref.shape[0]):
        total = total + moments_ref[k]
    moment = [total[k : k + 1] / total[:1] for k in range(6)]

    def inner(x, y, power):
        return sum(
            x[i] * y[j] * moment[i + j + power] for i in range(len(x)) for j in range(len(y))
        )

    one = jnp.ones_like(moment[0])
    residual, direction, effects = [one], [one], []
    norm_now = inner(residual, residual, 0)
    for step in range(3):
        step_size = norm_now / inner(direction, direction, 1)
        effects = [
            (effects[k] if k < len(effects) else 0.0) + step_size * direction[k] for k in range(len(direction))
        ]
        image = [0.0] + direction
        residual = [
            (residual[k] if k < len(residual) else 0.0) - step_size * image[k] for k in range(len(image))
        ]
        if step < 2:
            norm_next = inner(residual, residual, 0)
            ratio = norm_next / norm_now
            direction = [
                residual[k] + (ratio * direction[k] if k < len(direction) else 0.0) for k in range(len(residual))
            ]
            norm_now = norm_next
    rows = effects + residual
    table = jnp.concatenate(rows + [jnp.zeros((TILE - len(rows), total.shape[1]), f32)], axis=0).T
    table = table[: a_ref.shape[0]]
    col = [table[:, k : k + 1] for k in range(len(rows))]
    a, b, c, d = a_ref[...], b_ref[...], c_ref[...], d_ref[...]
    effects_ref[...] = col[0] * a + col[1] * b + col[2] * c
    residual_ref[...] = col[3] * a + col[4] * b + col[5] * c + col[6] * d


def shards(genotypes, z_scores):
    local_samples, variants = genotypes.shape
    blocks = lax.axis_size("genome")
    peers = lax.axis_size("cols")
    samples = local_samples * peers
    to_left = [(k + 1, k) for k in range(blocks - 1)]
    to_right = [(k, k + 1) for k in range(blocks - 1)]
    rows = TILE // peers

    near = peers // 2
    depth = NT * rows + 16
    cols = range(peers)
    sides = [list(cols[:near]), list(cols[near:])]

    half = variants // 2
    first = genotypes[:, :half].astype(bf16)
    next_first = lax.ppermute(first, "genome", to_left)
    second = lax.optimization_barrier((genotypes, first))[0][:, half:].astype(bf16)
    next_second = lax.ppermute(second, "genome", to_left)
    own = call(own_products, shape(near, 2 * depth, TILE, dtype=i16), first, second)
    own = lax.all_to_all(own, "cols", 0, 0, axis_index_groups=sides)
    head = call(head_products, shape(peers, 8 * rows, TILE, dtype=i16), first, second, next_first)
    keep, far = call(fold, (shape(depth, TILE, dtype=i32), shape(depth, TILE, dtype=i16)), own)
    z = z_scores.T
    vector = shape(*z.shape)
    code = shape(z.shape[0] // 16 * 16 + 16, z.shape[1], dtype=i16)
    z_code = call(start_code, code, z)
    far = lax.ppermute(far, "cols", [(k, (k + near) % peers) for k in cols])
    nxt = call(tail_products, shape(peers, depth, TILE, dtype=i16), second, next_second, head)
    z_code, nxt = lax.optimization_barrier((z_code, nxt))
    nxt = lax.all_to_all(nxt, "cols", 0, 0)
    z_next = lax.ppermute(z_code, "genome", to_left)
    codes, diagonal_row = call(
        functools.partial(correlate, samples),
        (shape(peers, SIDE * SIDE * rows, TILE, dtype=i16), shape(8, TILE)),
        keep,
        far,
        nxt,
    )
    codes = lax.all_to_all(codes, "cols", 0, 0)
    square = shape(W, W, dtype=bf16)
    near_h, near_l, next_h, next_l, back_h, back_l = call(unpack, (square,) * 6, codes, diagonal_row)

    inside = [(k, k ^ 1) for k in range(blocks)]
    across = [(k, ((k + 1) ^ 1) - 1) for k in range(1, blocks - 1)]

    def step(kernel, part, *came):
        w, out, inn = call(
            kernel, (vector, code, code), part, *came, back_h, back_l, next_h, next_l
        )
        out = lax.ppermute(out, "genome", across)
        inn = lax.ppermute(inn, "genome", inside)
        return w, call(inward, vector, w, near_h, near_l), out, inn

    came = lax.ppermute(call(outward, code, z, next_h, next_l), "genome", to_right)
    one, *rest = step(first_gather, call(inward, vector, z, near_h, near_l), came, z_next)
    two, part, out, inn = step(next_gather, *rest)
    early = call(early_moments, shape(8, 256), z, one, two)
    three, moments = call(
        last_vector, (vector, shape(blocks, 8, 256)), part, out, inn, back_h, back_l, two, early
    )
    moments = lax.all_to_all(moments, "genome", 0, 0)
    effects, residual = call(combine, (jax.ShapeDtypeStruct(z.shape, f32),) * 2, moments, z, one, two, three)
    return effects.T, residual.T


def solution(mesh):
    return jax.shard_map(
        shards,
        mesh=mesh,
        in_specs=(P("cols", "genome"), P("genome", "cols")),
        out_specs=(P("genome", "cols"), P("genome", "cols")),
        check_vma=False,
    )
```

```python
import functools

import jax
import jax.numpy as jnp
from jax import lax
from jax.experimental import pallas as pl
from jax.experimental.pallas import tpu as pltpu
from jax.sharding import PartitionSpec as P


W = 512
RIDGE = 0.1
FLOOR = 0.02
TILE = 128
SIDE = W // TILE
UPPER = tuple((p, q) for p in range(SIDE) for q in range(p, SIDE))
LOWER = tuple((p, q) for q in range(SIDE) for p in range(q, SIDE))
HEAD = tuple(t for t in LOWER if t[1] < SIDE // 2)
TAIL = tuple(t for t in LOWER if t[1] >= SIDE // 2)
NT = len(UPPER)
CODE = 32000.0
HALF = 32768
f32, bf16, i16, i32 = jnp.float32, jnp.bfloat16, jnp.int16, jnp.int32


def dot(a, b):
    return jnp.dot(a, b, preferred_element_type=f32)


def halves(a):
    high = a.astype(bf16)
    return high, (a - high.astype(f32)).astype(bf16)


def call(kernel, outs, *args):
    spec = pl.BlockSpec(memory_space=pltpu.VMEM)
    return pl.pallas_call(
        kernel,
        out_shape=outs,
        in_specs=[spec] * len(args),
        out_specs=jax.tree.map(lambda _: spec, outs, is_leaf=lambda o: not isinstance(o, tuple)),
        compiler_params=pltpu.CompilerParams(vmem_limit_bytes=16 << 20),
    )(*(pltpu.with_memory_space_constraint(a, pltpu.VMEM) for a in args))


def shape(*dims, dtype=f32):
    return pltpu.VMEM(dims, dtype)


def tile_of(matrix, p, q):
    return matrix[p * TILE : (p + 1) * TILE, q * TILE : (q + 1) * TILE]


def pack_tiles(tiles, block, peers, put):
    rows = TILE // peers
    pieces = [tile.reshape(peers, rows, TILE) for tile in tiles] + sums(block, peers, rows)
    for u in range(len(pieces) // 2):
        pair = jnp.concatenate(pieces[2 * u : 2 * u + 2], axis=1)
        put(2 * rows * u, pair.astype(i32).astype(i16))


def on_diagonal():
    return lax.broadcasted_iota(i32, (TILE, TILE), 0) == lax.broadcasted_iota(i32, (TILE, TILE), 1)


def sums(block, peers, rows):
    high = 0.0, 0.0
    step = 16
    for lo in range(0, block.shape[0], 60 * step):
        near = square = None
        for at in range(lo, min(lo + 60 * step, block.shape[0]), step):
            x = block[at : at + step]
            near, square = (x, x * x) if near is None else (near + x, square + x * x)
        high = high[0] + near.astype(f32), high[1] + square.astype(f32)
    both = [jnp.sum(v, axis=0, keepdims=True) for v in high]
    stats = [v[:, at : at + TILE] for v in both for at in range(0, block.shape[1], TILE)]
    if len(stats) < rows:
        stats.append(jnp.zeros((rows - len(stats), TILE), f32))
    stats = jnp.broadcast_to(jnp.concatenate(stats, axis=0)[None], (peers, rows, TILE))
    return [stats, jnp.zeros_like(stats)] if block.shape[1] == W else [stats]


def own_products(first_ref, second_ref, out_ref, turned_ref):
    block = jnp.concatenate([first_ref[...], second_ref[...]], axis=1)
    turned = block.T
    turned_ref[...] = turned[turned_ref.shape[0] :]
    near, depth = out_ref.shape[0], out_ref.shape[1] // 2
    peers = 2 * near

    def put(at, value):
        for far in range(2):
            lo = far * depth + at
            out_ref[:, lo : lo + value.shape[1], :] = value[far * near : (far + 1) * near]

    gram = dot(turned, block)
    pack_tiles([tile_of(gram, p, q) for p, q in UPPER], block, peers, put)


def head_products(first_ref, turned_ref, next_ref, out_ref):
    block = next_ref[...]
    grams = dot(first_ref[...].T, block), dot(turned_ref[...], block)

    def put(at, value):
        out_ref[:, at : at + value.shape[1], :] = value

    half = SIDE // 2
    pack_tiles([tile_of(grams[p // half], p % half, q) for p, q in HEAD], block, out_ref.shape[0], put)


def tail_products(turned_ref, next_ref, head_ref, out_ref):
    block = next_ref[...]
    gram = dot(turned_ref[...], block)
    done = head_ref.shape[1]
    out_ref[:, :done, :] = head_ref[...]

    def put(at, value):
        out_ref[:, done + at : done + at + value.shape[1], :] = value

    half = SIDE // 2
    pack_tiles([tile_of(gram, p - half, q - half) for p, q in TAIL], block, out_ref.shape[0], put)


def fold(came_ref, keep_ref, send_ref):
    near, depth = came_ref.shape[0], came_ref.shape[1] // 2
    far = lax.axis_index("cols") // near

    def total(side):
        rows = pl.ds(pl.multiple_of(side * depth, depth), depth)
        acc = came_ref[0, rows, :].astype(i32)
        for k in range(1, near):
            acc = acc + came_ref[k, rows, :].astype(i32)
        return acc

    keep_ref[...] = total(far)
    send_ref[...] = (total(1 - far) - HALF).astype(i16)


def correlate(samples, keep_ref, far_ref, next_ref, out_ref, diagonal_ref):
    peers = next_ref.shape[0]
    rows = TILE // peers
    own = keep_ref[...] + far_ref[...].astype(i32) + HALF
    nxt = next_ref[0].astype(i32)
    for k in range(1, peers):
        nxt = nxt + next_ref[k].astype(i32)
    own, nxt = own.astype(f32) / samples, nxt.astype(f32) / samples

    def stats(means):
        mean, square = means[:SIDE], means[SIDE : 2 * SIDE]
        variance = square - mean * mean
        return mean, variance, 1.0 / jnp.sqrt(jnp.maximum(variance, FLOOR))

    mean, variance, scale = stats(own[NT * rows :])
    slot = {tile: t for t, tile in enumerate(HEAD + ("head",) + TAIL + ("tail",))}
    half = SIDE // 2
    parts = [nxt[slot[name] * rows : slot[name] * rows + SIDE] for name in ("head", "tail")]
    next_mean, _, next_scale = stats(jnp.concatenate([v[k : k + half] for k in (0, half) for v in parts], axis=0))
    diagonal_ref[...] = jnp.concatenate([variance * scale * scale, jnp.zeros((8 - SIDE, TILE), f32)], axis=0)
    lane = lax.broadcasted_iota(i32, (rows, TILE), 1)
    row = lax.broadcasted_iota(i32, (rows, TILE), 0) + lax.axis_index("cols") * rows

    def at_rows(vector, p):
        return jnp.sum(jnp.where(lane == row, vector[p : p + 1], 0.0), axis=1, keepdims=True)

    row_mean = [at_rows(mean, p) for p in range(SIDE)]
    row_scale = [at_rows(scale, p) * CODE for p in range(SIDE)]

    def code(means, t, p, q, col_mean, col_scale):
        cov = means[t * rows : (t + 1) * rows] - row_mean[p] * col_mean[q : q + 1]
        return jnp.round(cov * row_scale[p] * col_scale[q : q + 1])

    upper = {(p, q): code(own, t, p, q, mean, scale) for t, (p, q) in enumerate(UPPER)}
    lower = {(p, q): code(nxt, slot[p, q], p, q, next_mean, next_scale) for p, q in LOWER}
    codes = []
    for p in range(SIDE):
        for q in range(SIDE):
            if p == q:
                codes.append(jnp.where(lane > row, upper[p, q], lower[p, q]))
            else:
                codes.append(upper[p, q] if p < q else lower[p, q])
    codes = jnp.concatenate(codes, axis=0).astype(i32).astype(i16)
    for k in range(peers):
        out_ref[k] = codes


def taper(p, q, shift):
    row = lax.broadcasted_iota(i32, (TILE, TILE), 0) + p * TILE
    col = lax.broadcasted_iota(i32, (TILE, TILE), 1) + q * TILE + shift
    reach = jnp.abs(col - row).astype(f32)
    return jnp.maximum(1.0 - reach / (W + 1), 0.0)


def unpack(codes_ref, diagonal_ref, v_ref, near_high, near_low, next_high, next_low, back_high, back_low, out_ref):
    peers = codes_ref.shape[0]
    rows = TILE // peers

    def put(high_ref, low_ref, p, q, value):
        high, low = halves(value)
        high_ref[p * TILE : (p + 1) * TILE, q * TILE : (q + 1) * TILE] = high
        low_ref[p * TILE : (p + 1) * TILE, q * TILE : (q + 1) * TILE] = low

    def put_near(p, q, code):
        value = code * (taper(p, q, 0) * (1.0 / CODE))
        if p == q:
            value = value + value.T
            value = jnp.where(on_diagonal(), diagonal_ref[p : p + 1, :], value)
            put(near_high, near_low, p, q, value)
        else:
            put(near_high, near_low, p, q, value)
            put(near_high, near_low, q, p, value.T)

    def put_next(p, q, code):
        value = code * (taper(p, q, W) * (1.0 / CODE))
        put(next_high, next_low, p, q, value)
        put(back_high, back_low, q, p, value.T)

    strict = lax.broadcasted_iota(i32, (TILE, TILE), 0) < lax.broadcasted_iota(i32, (TILE, TILE), 1)
    zero = jnp.zeros((TILE, TILE), f32)
    for p in range(SIDE):
        for u in range(SIDE // 2):
            lo = 2 * rows * (p * SIDE // 2 + u)
            pair = codes_ref[:, lo : lo + 2 * rows, :].astype(i32).astype(f32)
            for q, code in ((2 * u, pair[:, :rows]), (2 * u + 1, pair[:, rows:])):
                code = code.reshape(TILE, TILE)
                if p <= q:
                    put_near(p, q, jnp.where(strict, code, 0.0) if p == q else code)
                if p >= q:
                    put_next(p, q, code)
                else:
                    put(next_high, next_low, p, q, zero)
                    put(back_high, back_low, q, p, zero)
    encode(product(v_ref[...], next_high, next_low), out_ref)


def product(v, high_ref, low_ref):
    high, low = halves(v)
    return dot(high, high_ref[...]) + dot(low, high_ref[...]) + dot(high, low_ref[...])


def diagonal(rows):
    return lax.broadcasted_iota(i32, (rows, 256), 0) == lax.broadcasted_iota(i32, (rows, 256), 1)


def encode(v, out_ref):
    rows = v.shape[0]
    top = jnp.max(jnp.abs(v), axis=1, keepdims=True)
    power = jnp.ceil(jnp.log2(jnp.maximum(top, 1e-30)) + 0.01)
    code = jnp.round(v * (jnp.exp2(-power) * CODE))
    turned = jnp.sum(jnp.where(diagonal(rows), power, 0.0), axis=0, keepdims=True)
    tail = jnp.broadcast_to(jnp.concatenate([turned, turned], axis=1), (out_ref.shape[0] - rows, v.shape[1]))
    out_ref[...] = jnp.concatenate([code, tail], axis=0).astype(i32).astype(i16)


def decode(code, rows):
    code = code.astype(i32).astype(f32)
    power = jnp.sum(jnp.where(diagonal(rows), code[rows : rows + 1, :256], 0.0), axis=1, keepdims=True)
    return code[:rows] * (jnp.exp2(power) * (1.0 / CODE))


def start_code(v_ref, out_ref):
    encode(v_ref[...], out_ref)


def inward(v_ref, high_ref, low_ref, out_ref):
    out_ref[...] = product(v_ref[...], high_ref, low_ref) + RIDGE * v_ref[...]


def gather(part_ref, came, nxt, back_h, back_l):
    rows = part_ref.shape[0]
    return part_ref[...] + decode(came, rows) + product(decode(nxt, rows), back_h, back_l)


def first_gather(part_ref, came_ref, next_ref, back_h, back_l, next_h, next_l, out_ref, across_ref, inside_ref):
    w = gather(part_ref, came_ref[...], next_ref[...], back_h, back_l)
    hand_on(w, next_h, next_l, out_ref, across_ref, inside_ref)


def next_gather(part_ref, across_in, inside_in, back_h, back_l, next_h, next_l, out_ref, across_ref, inside_ref):
    w = gather(part_ref, *arrived(across_in, inside_in), back_h, back_l)
    hand_on(w, next_h, next_l, out_ref, across_ref, inside_ref)


def odd():
    return lax.rem(lax.axis_index("genome"), 2)


def hand_on(w, next_h, next_l, out_ref, across_ref, inside_ref):
    out_ref[...] = w

    @pl.when(odd() == 0)
    def _():
        encode(w, across_ref)
        encode(product(w, next_h, next_l), inside_ref)

    @pl.when(odd() == 1)
    def _():
        encode(product(w, next_h, next_l), across_ref)
        encode(w, inside_ref)


def arrived(across_in, inside_in):
    even = odd() == 0
    across, inside = across_in[...].astype(i32), inside_in[...].astype(i32)
    return jnp.where(even, across, inside), jnp.where(even, inside, across)


def along(a, b):
    return jnp.sum(a * b, axis=1, keepdims=True)


def turn(moment):
    return jnp.sum(jnp.where(diagonal(moment.shape[0]), moment, 0.0), axis=0, keepdims=True)


def early_moments(a_ref, b_ref, c_ref, out_ref):
    a, b, c = a_ref[...], b_ref[...], c_ref[...]
    rows = [turn(m) for m in (along(a, a), along(a, b), along(b, b), along(b, c), along(c, c))]
    out_ref[...] = jnp.concatenate(rows + [jnp.zeros((3, 256), f32)], axis=0)


def last_vector(part_ref, across_in, inside_in, back_h, back_l, c_ref, early_ref, out_ref, moments_ref):
    w = gather(part_ref, *arrived(across_in, inside_in), back_h, back_l)
    out_ref[...] = w
    row = lax.broadcasted_iota(i32, early_ref.shape, 0)
    moments = jnp.where(row == 5, turn(along(c_ref[...], w)), early_ref[...])
    for k in range(moments_ref.shape[0]):
        moments_ref[k] = moments


def combine(moments_ref, a_ref, b_ref, c_ref, d_ref, effects_ref, residual_ref):
    total = moments_ref[0]
    for k in range(1, moments_ref.shape[0]):
        total = total + moments_ref[k]
    moment = [total[k : k + 1] / total[:1] for k in range(6)]

    def inner(x, y, power):
        return sum(
            x[i] * y[j] * moment[i + j + power] for i in range(len(x)) for j in range(len(y))
        )

    one = jnp.ones_like(moment[0])
    residual, direction, effects = [one], [one], []
    norm_now = inner(residual, residual, 0)
    for step in range(3):
        step_size = norm_now / inner(direction, direction, 1)
        effects = [
            (effects[k] if k < len(effects) else 0.0) + step_size * direction[k] for k in range(len(direction))
        ]
        image = [0.0] + direction
        residual = [
            (residual[k] if k < len(residual) else 0.0) - step_size * image[k] for k in range(len(image))
        ]
        if step < 2:
            norm_next = inner(residual, residual, 0)
            ratio = norm_next / norm_now
            direction = [
                residual[k] + (ratio * direction[k] if k < len(direction) else 0.0) for k in range(len(residual))
            ]
            norm_now = norm_next
    rows = effects + residual
    table = jnp.concatenate(rows + [jnp.zeros((TILE - len(rows), total.shape[1]), f32)], axis=0).T
    table = table[: a_ref.shape[0]]
    col = [table[:, k : k + 1] for k in range(len(rows))]
    a, b, c, d = a_ref[...], b_ref[...], c_ref[...], d_ref[...]
    effects_ref[...] = col[0] * a + col[1] * b + col[2] * c
    residual_ref[...] = col[3] * a + col[4] * b + col[5] * c + col[6] * d


def shards(genotypes, z_scores):
    local_samples, variants = genotypes.shape
    blocks = lax.axis_size("genome")
    peers = lax.axis_size("cols")
    samples = local_samples * peers
    to_left = [(k + 1, k) for k in range(blocks - 1)]
    to_right = [(k, k + 1) for k in range(blocks - 1)]
    rows = TILE // peers

    near = peers // 2
    depth = NT * rows + 16
    cols = range(peers)
    sides = [list(cols[:near]), list(cols[near:])]

    half = variants // 2
    first = genotypes[:, :half].astype(bf16)
    next_first = lax.ppermute(first, "genome", to_left)
    second = lax.optimization_barrier((genotypes, first))[0][:, half:].astype(bf16)
    next_second = lax.ppermute(second, "genome", to_left)
    own, turned = call(
        own_products,
        (jax.ShapeDtypeStruct((near, 2 * depth, TILE), i16), shape(half, local_samples, dtype=bf16)),
        first,
        second,
    )
    own = lax.all_to_all(own, "cols", 0, 0, axis_index_groups=sides)
    head = call(head_products, shape(peers, 8 * rows, TILE, dtype=i16), first, turned, next_first)
    keep, far = call(fold, (shape(depth, TILE, dtype=i32), shape(depth, TILE, dtype=i16)), own)
    z = z_scores.T
    vector = shape(*z.shape)
    code = shape(z.shape[0] // 16 * 16 + 16, z.shape[1], dtype=i16)
    z_code = call(start_code, code, z)
    far = lax.ppermute(far, "cols", [(k, (k + near) % peers) for k in cols])
    nxt = call(tail_products, shape(peers, depth, TILE, dtype=i16), turned, next_second, head)
    nxt = lax.all_to_all(nxt, "cols", 0, 0)
    z_next = lax.ppermute(z_code, "genome", to_left)
    codes, diagonal_row = call(
        functools.partial(correlate, samples),
        (shape(peers, SIDE * SIDE * rows, TILE, dtype=i16), shape(8, TILE)),
        keep,
        far,
        nxt,
    )
    codes, z_next = lax.optimization_barrier((codes, z_next))
    codes = lax.all_to_all(codes, "cols", 0, 0)
    square = shape(W, W, dtype=bf16)
    near_h, near_l, next_h, next_l, back_h, back_l, out = call(unpack, (square,) * 6 + (code,), codes, diagonal_row, z)

    inside = [(k, k ^ 1) for k in range(blocks)]
    across = [(k, ((k + 1) ^ 1) - 1) for k in range(1, blocks - 1)]

    def step(kernel, part, *came):
        w, out, inn = call(
            kernel, (vector, code, code), part, *came, back_h, back_l, next_h, next_l
        )
        out = lax.ppermute(out, "genome", across)
        inn = lax.ppermute(inn, "genome", inside)
        return w, call(inward, vector, w, near_h, near_l), out, inn

    came = lax.ppermute(out, "genome", to_right)
    one, *rest = step(first_gather, call(inward, vector, z, near_h, near_l), came, z_next)
    two, part, out, inn = step(next_gather, *rest)
    early = call(early_moments, shape(8, 256), z, one, two)
    three, moments = call(
        last_vector, (vector, shape(blocks, 8, 256)), part, out, inn, back_h, back_l, two, early
    )
    moments = lax.all_to_all(moments, "genome", 0, 0)
    effects, residual = call(combine, (jax.ShapeDtypeStruct(z.shape, f32),) * 2, moments, z, one, two, three)
    return effects.T, residual.T


def solution(mesh):
    return jax.shard_map(
        shards,
        mesh=mesh,
        in_specs=(P("cols", "genome"), P("genome", "cols")),
        out_specs=(P("genome", "cols"), P("genome", "cols")),
        check_vma=False,
    )
```

```python
import functools

import jax
import jax.numpy as jnp
from jax import lax
from jax.experimental import pallas as pl
from jax.experimental.pallas import tpu as pltpu
from jax.sharding import PartitionSpec as P


W = 512
RIDGE = 0.1
FLOOR = 0.02
TILE = 128
SIDE = W // TILE
UPPER = tuple((p, q) for p in range(SIDE) for q in range(p, SIDE))
LOWER = tuple((p, q) for q in range(SIDE) for p in range(q, SIDE))
HEAD = tuple(t for t in LOWER if t[1] < SIDE // 2)
TAIL = tuple(t for t in LOWER if t[1] >= SIDE // 2)
NT = len(UPPER)
CODE = 32000.0
SLOT = 192
HALF = 32768
f32, bf16, i16, i32 = jnp.float32, jnp.bfloat16, jnp.int16, jnp.int32


def dot(a, b):
    return jnp.dot(a, b, preferred_element_type=f32)


def halves(a):
    high = a.astype(bf16)
    return high, (a - high.astype(f32)).astype(bf16)


def call(kernel, outs, *args):
    spec = pl.BlockSpec(memory_space=pltpu.VMEM)
    return pl.pallas_call(
        kernel,
        out_shape=outs,
        in_specs=[spec] * len(args),
        out_specs=jax.tree.map(lambda _: spec, outs, is_leaf=lambda o: not isinstance(o, tuple)),
        compiler_params=pltpu.CompilerParams(vmem_limit_bytes=16 << 20),
    )(*(pltpu.with_memory_space_constraint(a, pltpu.VMEM) for a in args))


def shape(*dims, dtype=f32):
    return pltpu.VMEM(dims, dtype)


def tile_of(matrix, p, q):
    return matrix[p * TILE : (p + 1) * TILE, q * TILE : (q + 1) * TILE]


def pack_tiles(tiles, block, peers, put):
    rows = TILE // peers
    pieces = [tile.reshape(peers, rows, TILE) for tile in tiles] + sums(block, peers, rows)
    for u in range(len(pieces) // 2):
        pair = jnp.concatenate(pieces[2 * u : 2 * u + 2], axis=1)
        put(2 * rows * u, pair.astype(i32).astype(i16))


def on_diagonal():
    return lax.broadcasted_iota(i32, (TILE, TILE), 0) == lax.broadcasted_iota(i32, (TILE, TILE), 1)


def sums(block, peers, rows):
    high = 0.0, 0.0
    step = 16
    for lo in range(0, block.shape[0], 60 * step):
        near = square = None
        for at in range(lo, min(lo + 60 * step, block.shape[0]), step):
            x = block[at : at + step]
            near, square = (x, x * x) if near is None else (near + x, square + x * x)
        high = high[0] + near.astype(f32), high[1] + square.astype(f32)
    both = [jnp.sum(v, axis=0, keepdims=True) for v in high]
    stats = [v[:, at : at + TILE] for v in both for at in range(0, block.shape[1], TILE)]
    if len(stats) < rows:
        stats.append(jnp.zeros((rows - len(stats), TILE), f32))
    stats = jnp.broadcast_to(jnp.concatenate(stats, axis=0)[None], (peers, rows, TILE))
    return [stats, jnp.zeros_like(stats)] if block.shape[1] == W else [stats]


def own_products(first_ref, second_ref, out_ref, turned_ref):
    block = jnp.concatenate([first_ref[...], second_ref[...]], axis=1)
    turned = block.T
    turned_ref[...] = turned[turned_ref.shape[0] :]
    near, depth = out_ref.shape[0], out_ref.shape[1] // 2
    peers = 2 * near

    def put(at, value):
        for far in range(2):
            lo = far * depth + at
            out_ref[:, lo : lo + value.shape[1], :] = value[far * near : (far + 1) * near]

    gram = dot(turned, block)
    pack_tiles([tile_of(gram, p, q) for p, q in UPPER], block, peers, put)


def head_products(first_ref, turned_ref, next_ref, out_ref):
    block = next_ref[...]
    grams = dot(first_ref[...].T, block), dot(turned_ref[...], block)

    def put(at, value):
        out_ref[:, at : at + value.shape[1], :] = value

    half = SIDE // 2
    pack_tiles([tile_of(grams[p // half], p % half, q) for p, q in HEAD], block, out_ref.shape[0], put)


def tail_products(turned_ref, next_ref, head_ref, out_ref):
    block = next_ref[...]
    gram = dot(turned_ref[...], block)
    done = head_ref.shape[1]
    out_ref[:, :done, :] = head_ref[...]

    def put(at, value):
        out_ref[:, done + at : done + at + value.shape[1], :] = value

    half = SIDE // 2
    pack_tiles([tile_of(gram, p - half, q - half) for p, q in TAIL], block, out_ref.shape[0], put)


def fold(came_ref, keep_ref, send_ref):
    near, depth = came_ref.shape[0], came_ref.shape[1] // 2
    far = lax.axis_index("cols") // near

    def total(side):
        rows = pl.ds(pl.multiple_of(side * depth, depth), depth)
        acc = came_ref[0, rows, :].astype(i32)
        for k in range(1, near):
            acc = acc + came_ref[k, rows, :].astype(i32)
        return acc

    keep_ref[...] = total(far)
    send_ref[...] = (total(1 - far) - HALF).astype(i16)


def correlate(samples, keep_ref, far_ref, next_ref, out_ref, diagonal_ref):
    peers = next_ref.shape[0]
    rows = TILE // peers
    own = keep_ref[...] + far_ref[...].astype(i32) + HALF
    nxt = next_ref[0].astype(i32)
    for k in range(1, peers):
        nxt = nxt + next_ref[k].astype(i32)
    own, nxt = own.astype(f32) / samples, nxt.astype(f32) / samples

    def stats(means):
        mean, square = means[:SIDE], means[SIDE : 2 * SIDE]
        variance = square - mean * mean
        return mean, variance, 1.0 / jnp.sqrt(jnp.maximum(variance, FLOOR))

    mean, variance, scale = stats(own[NT * rows :])
    slot = {tile: t for t, tile in enumerate(HEAD + ("head",) + TAIL + ("tail",))}
    half = SIDE // 2
    parts = [nxt[slot[name] * rows : slot[name] * rows + SIDE] for name in ("head", "tail")]
    next_mean, _, next_scale = stats(jnp.concatenate([v[k : k + half] for k in (0, half) for v in parts], axis=0))
    diagonal_ref[...] = jnp.concatenate([variance * scale * scale, jnp.zeros((8 - SIDE, TILE), f32)], axis=0)
    lane = lax.broadcasted_iota(i32, (rows, TILE), 1)
    row = lax.broadcasted_iota(i32, (rows, TILE), 0) + lax.axis_index("cols") * rows

    def at_rows(vector, p):
        return jnp.sum(jnp.where(lane == row, vector[p : p + 1], 0.0), axis=1, keepdims=True)

    row_mean = [at_rows(mean, p) for p in range(SIDE)]
    row_scale = [at_rows(scale, p) * CODE for p in range(SIDE)]

    def code(means, t, p, q, col_mean, col_scale):
        cov = means[t * rows : (t + 1) * rows] - row_mean[p] * col_mean[q : q + 1]
        return jnp.round(cov * row_scale[p] * col_scale[q : q + 1])

    upper = {(p, q): code(own, t, p, q, mean, scale) for t, (p, q) in enumerate(UPPER)}
    lower = {(p, q): code(nxt, slot[p, q], p, q, next_mean, next_scale) for p, q in LOWER}
    codes = []
    for p in range(SIDE):
        for q in range(SIDE):
            if p == q:
                codes.append(jnp.where(lane > row, upper[p, q], lower[p, q]))
            else:
                codes.append(upper[p, q] if p < q else lower[p, q])
    codes = jnp.concatenate(codes, axis=0).astype(i32).astype(i16)
    for k in range(peers):
        out_ref[k] = codes


def taper(p, q, shift):
    row = lax.broadcasted_iota(i32, (TILE, TILE), 0) + p * TILE
    col = lax.broadcasted_iota(i32, (TILE, TILE), 1) + q * TILE + shift
    reach = jnp.abs(col - row).astype(f32)
    return jnp.maximum(1.0 - reach / (W + 1), 0.0)


def unpack(codes_ref, diagonal_ref, v_ref, near_high, near_low, next_high, next_low, back_high, back_low, out_ref):
    peers = codes_ref.shape[0]
    rows = TILE // peers

    def put(high_ref, low_ref, p, q, value):
        high, low = halves(value)
        high_ref[p * TILE : (p + 1) * TILE, q * TILE : (q + 1) * TILE] = high
        low_ref[p * TILE : (p + 1) * TILE, q * TILE : (q + 1) * TILE] = low

    def put_near(p, q, code):
        value = code * (taper(p, q, 0) * (1.0 / CODE))
        if p == q:
            value = value + value.T
            value = jnp.where(on_diagonal(), diagonal_ref[p : p + 1, :], value)
            put(near_high, near_low, p, q, value)
        else:
            put(near_high, near_low, p, q, value)
            put(near_high, near_low, q, p, value.T)

    def put_next(p, q, code):
        value = code * (taper(p, q, W) * (1.0 / CODE))
        put(next_high, next_low, p, q, value)
        put(back_high, back_low, q, p, value.T)

    strict = lax.broadcasted_iota(i32, (TILE, TILE), 0) < lax.broadcasted_iota(i32, (TILE, TILE), 1)
    zero = jnp.zeros((TILE, TILE), f32)
    for p in range(SIDE):
        for u in range(SIDE // 2):
            lo = 2 * rows * (p * SIDE // 2 + u)
            pair = codes_ref[:, lo : lo + 2 * rows, :].astype(i32).astype(f32)
            for q, code in ((2 * u, pair[:, :rows]), (2 * u + 1, pair[:, rows:])):
                code = code.reshape(TILE, TILE)
                if p <= q:
                    put_near(p, q, jnp.where(strict, code, 0.0) if p == q else code)
                if p >= q:
                    put_next(p, q, code)
                else:
                    put(next_high, next_low, p, q, zero)
                    put(back_high, back_low, q, p, zero)
    encode(product(v_ref[...], next_high, next_low), out_ref)


def product(v, high_ref, low_ref):
    high, low = halves(v)
    return dot(high, high_ref[...]) + dot(low, high_ref[...]) + dot(high, low_ref[...])


def diagonal(rows):
    return lax.broadcasted_iota(i32, (rows, 256), 0) == lax.broadcasted_iota(i32, (rows, 256), 1)


def encode(v, out_ref):
    rows = v.shape[0]
    top = jnp.max(jnp.abs(v), axis=1, keepdims=True)
    power = jnp.ceil(jnp.log2(jnp.maximum(top, 1e-30)) + 0.01)
    code = jnp.round(v * (jnp.exp2(-power) * CODE))
    turned = jnp.sum(jnp.where(diagonal(rows), power, 0.0), axis=0, keepdims=True)
    tail = jnp.broadcast_to(jnp.concatenate([turned, turned], axis=1), (out_ref.shape[0] - rows, v.shape[1]))
    out_ref[...] = jnp.concatenate([code, tail], axis=0).astype(i32).astype(i16)


def decode(code, rows):
    code = code.astype(i32).astype(f32)
    power = jnp.sum(jnp.where(diagonal(rows), code[rows : rows + 1, :256], 0.0), axis=1, keepdims=True)
    return code[:rows] * (jnp.exp2(power) * (1.0 / CODE))


def start_code(v_ref, out_ref):
    encode(v_ref[...], out_ref)


def inward(v_ref, high_ref, low_ref, out_ref):
    out_ref[...] = product(v_ref[...], high_ref, low_ref) + RIDGE * v_ref[...]


def gather(part_ref, came, nxt, back_h, back_l):
    rows = part_ref.shape[0]
    return part_ref[...] + decode(came, rows) + product(decode(nxt, rows), back_h, back_l)


def first_gather(part_ref, came_ref, next_ref, back_h, back_l, next_h, next_l, out_ref, across_ref, inside_ref):
    w = gather(part_ref, came_ref[...], next_ref[...], back_h, back_l)
    hand_on(w, next_h, next_l, out_ref, across_ref, inside_ref)


def next_gather(part_ref, across_in, inside_in, back_h, back_l, next_h, next_l, out_ref, across_ref, inside_ref):
    w = gather(part_ref, *arrived(across_in, inside_in), back_h, back_l)
    hand_on(w, next_h, next_l, out_ref, across_ref, inside_ref)


def odd():
    return lax.rem(lax.axis_index("genome"), 2)


def hand_on(w, next_h, next_l, out_ref, across_ref, inside_ref):
    out_ref[...] = w

    @pl.when(odd() == 0)
    def _():
        encode(w, across_ref)
        encode(product(w, next_h, next_l), inside_ref)

    @pl.when(odd() == 1)
    def _():
        encode(product(w, next_h, next_l), across_ref)
        encode(w, inside_ref)


def arrived(across_in, inside_in):
    even = odd() == 0
    across, inside = across_in[...].astype(i32), inside_in[...].astype(i32)
    return jnp.where(even, across, inside), jnp.where(even, inside, across)


def along(a, b):
    return jnp.sum(a * b, axis=1, keepdims=True)


def turn(moment):
    return jnp.sum(jnp.where(diagonal(moment.shape[0]), moment, 0.0), axis=0, keepdims=True)


def early_moments(a_ref, b_ref, c_ref, out_ref):
    a, b, c = a_ref[...], b_ref[...], c_ref[...]
    rows = [turn(m) for m in (along(a, a), along(a, b), along(b, b), along(b, c), along(c, c))]
    out_ref[...] = jnp.concatenate(rows + [jnp.zeros((3, 256), f32)], axis=0)


def last_vector(part_ref, across_in, inside_in, back_h, back_l, c_ref, early_ref, out_ref, moments_ref):
    w = gather(part_ref, *arrived(across_in, inside_in), back_h, back_l)
    out_ref[...] = w
    early = early_ref[...]
    rows = [early[k : k + 1, :SLOT] for k in range(5)] + [turn(along(c_ref[...], w))[:, :SLOT]]
    fill = moments_ref.shape[2] - 6 * SLOT
    moments = jnp.concatenate(rows + [jnp.zeros((1, fill), f32)], axis=1)
    for k in range(moments_ref.shape[0]):
        moments_ref[k] = moments


def combine(moments_ref, a_ref, b_ref, c_ref, d_ref, effects_ref, residual_ref):
    total = moments_ref[0]
    for k in range(1, moments_ref.shape[0]):
        total = total + moments_ref[k]
    first = total[:, :256]
    moment = [total[:, k * SLOT : k * SLOT + 256] / first for k in range(6)]

    def inner(x, y, power):
        return sum(
            x[i] * y[j] * moment[i + j + power] for i in range(len(x)) for j in range(len(y))
        )

    one = jnp.ones_like(moment[0])
    residual, direction, effects = [one], [one], []
    norm_now = inner(residual, residual, 0)
    for step in range(3):
        step_size = norm_now / inner(direction, direction, 1)
        effects = [
            (effects[k] if k < len(effects) else 0.0) + step_size * direction[k] for k in range(len(direction))
        ]
        image = [0.0] + direction
        residual = [
            (residual[k] if k < len(residual) else 0.0) - step_size * image[k] for k in range(len(image))
        ]
        if step < 2:
            norm_next = inner(residual, residual, 0)
            ratio = norm_next / norm_now
            direction = [
                residual[k] + (ratio * direction[k] if k < len(direction) else 0.0) for k in range(len(residual))
            ]
            norm_now = norm_next
    rows = effects + residual
    table = jnp.concatenate(rows + [jnp.zeros((TILE - len(rows), 256), f32)], axis=0).T
    table = table[: a_ref.shape[0]]
    col = [table[:, k : k + 1] for k in range(len(rows))]
    a, b, c, d = a_ref[...], b_ref[...], c_ref[...], d_ref[...]
    effects_ref[...] = col[0] * a + col[1] * b + col[2] * c
    residual_ref[...] = col[3] * a + col[4] * b + col[5] * c + col[6] * d


def shards(genotypes, z_scores):
    local_samples, variants = genotypes.shape
    blocks = lax.axis_size("genome")
    peers = lax.axis_size("cols")
    samples = local_samples * peers
    to_left = [(k + 1, k) for k in range(blocks - 1)]
    to_right = [(k, k + 1) for k in range(blocks - 1)]
    rows = TILE // peers

    near = peers // 2
    depth = NT * rows + 16
    cols = range(peers)
    sides = [list(cols[:near]), list(cols[near:])]

    half = variants // 2
    first = genotypes[:, :half].astype(bf16)
    next_first = lax.ppermute(first, "genome", to_left)
    second = lax.optimization_barrier((genotypes, first))[0][:, half:].astype(bf16)
    next_second = lax.ppermute(second, "genome", to_left)
    own, turned = call(
        own_products,
        (jax.ShapeDtypeStruct((near, 2 * depth, TILE), i16), shape(half, local_samples, dtype=bf16)),
        first,
        second,
    )
    own = lax.all_to_all(own, "cols", 0, 0, axis_index_groups=sides)
    head = call(head_products, shape(peers, 8 * rows, TILE, dtype=i16), first, turned, next_first)
    keep, far = call(fold, (shape(depth, TILE, dtype=i32), shape(depth, TILE, dtype=i16)), own)
    z = z_scores.T
    vector = shape(*z.shape)
    code = shape(z.shape[0] // 16 * 16 + 16, z.shape[1], dtype=i16)
    z_code = call(start_code, code, z)
    far = lax.ppermute(far, "cols", [(k, (k + near) % peers) for k in cols])
    nxt = call(tail_products, shape(peers, depth, TILE, dtype=i16), turned, next_second, head)
    nxt = lax.all_to_all(nxt, "cols", 0, 0)
    z_next = lax.ppermute(z_code, "genome", to_left)
    codes, diagonal_row = call(
        functools.partial(correlate, samples),
        (shape(peers, SIDE * SIDE * rows, TILE, dtype=i16), shape(8, TILE)),
        keep,
        far,
        nxt,
    )
    codes, z_next = lax.optimization_barrier((codes, z_next))
    codes = lax.all_to_all(codes, "cols", 0, 0)
    square = shape(W, W, dtype=bf16)
    near_h, near_l, next_h, next_l, back_h, back_l, out = call(unpack, (square,) * 6 + (code,), codes, diagonal_row, z)

    inside = [(k, k ^ 1) for k in range(blocks)]
    across = [(k, ((k + 1) ^ 1) - 1) for k in range(1, blocks - 1)]

    def step(kernel, part, *came):
        w, out, inn = call(
            kernel, (vector, code, code), part, *came, back_h, back_l, next_h, next_l
        )
        out = lax.ppermute(out, "genome", across)
        inn = lax.ppermute(inn, "genome", inside)
        return w, call(inward, vector, w, near_h, near_l), out, inn

    came = lax.ppermute(out, "genome", to_right)
    one, *rest = step(first_gather, call(inward, vector, z, near_h, near_l), came, z_next)
    two, part, out, inn = step(next_gather, *rest)
    early = call(early_moments, shape(8, 256), z, one, two)
    three, moments = call(
        last_vector, (vector, shape(blocks, 1, 1280)), part, out, inn, back_h, back_l, two, early
    )
    moments = lax.all_to_all(moments, "genome", 0, 0)
    effects, residual = call(combine, (jax.ShapeDtypeStruct(z.shape, f32),) * 2, moments, z, one, two, three)
    return effects.T, residual.T


def solution(mesh):
    return jax.shard_map(
        shards,
        mesh=mesh,
        in_specs=(P("cols", "genome"), P("genome", "cols")),
        out_specs=(P("genome", "cols"), P("genome", "cols")),
        check_vma=False,
    )
```

```python
import functools

import jax
import jax.numpy as jnp
from jax import lax
from jax.experimental import pallas as pl
from jax.experimental.pallas import tpu as pltpu
from jax.sharding import PartitionSpec as P


W = 512
RIDGE = 0.1
FLOOR = 0.02
TILE = 128
SIDE = W // TILE
UPPER = tuple((p, q) for p in range(SIDE) for q in range(p, SIDE))
LOWER = tuple((p, q) for q in range(SIDE) for p in range(q, SIDE))
HEAD = tuple(t for t in LOWER if t[1] < SIDE // 2)
TAIL = tuple(t for t in LOWER if t[1] >= SIDE // 2)
NT = len(UPPER)
CODE = 32000.0
SLOT = 192
HALF = 32768
f32, bf16, i16, i32 = jnp.float32, jnp.bfloat16, jnp.int16, jnp.int32


def dot(a, b):
    return jnp.dot(a, b, preferred_element_type=f32)


def halves(a):
    high = a.astype(bf16)
    return high, (a - high.astype(f32)).astype(bf16)


def call(kernel, outs, *args):
    spec = pl.BlockSpec(memory_space=pltpu.VMEM)
    return pl.pallas_call(
        kernel,
        out_shape=outs,
        in_specs=[spec] * len(args),
        out_specs=jax.tree.map(lambda _: spec, outs, is_leaf=lambda o: not isinstance(o, tuple)),
        compiler_params=pltpu.CompilerParams(vmem_limit_bytes=16 << 20),
    )(*(pltpu.with_memory_space_constraint(a, pltpu.VMEM) for a in args))


def shape(*dims, dtype=f32):
    return pltpu.VMEM(dims, dtype)


def tile_of(matrix, p, q):
    return matrix[p * TILE : (p + 1) * TILE, q * TILE : (q + 1) * TILE]


def pack_tiles(tiles, block, peers, put):
    rows = TILE // peers
    pieces = [tile.reshape(peers, rows, TILE) for tile in tiles]
    if block is not None:
        pieces += sums(block, peers, rows)
    for u in range((len(pieces) + 1) // 2):
        pair = jnp.concatenate(pieces[2 * u : 2 * u + 2], axis=1)
        put(2 * rows * u, pair.astype(i32).astype(i16))


def on_diagonal():
    return lax.broadcasted_iota(i32, (TILE, TILE), 0) == lax.broadcasted_iota(i32, (TILE, TILE), 1)


def sums(block, peers, rows):
    high = 0.0, 0.0
    step = 16
    for lo in range(0, block.shape[0], 60 * step):
        near = square = None
        for at in range(lo, min(lo + 60 * step, block.shape[0]), step):
            x = block[at : at + step]
            near, square = (x, x * x) if near is None else (near + x, square + x * x)
        high = high[0] + near.astype(f32), high[1] + square.astype(f32)
    both = [jnp.sum(v, axis=0, keepdims=True) for v in high]
    stats = [v[:, at : at + TILE] for v in both for at in range(0, block.shape[1], TILE)]
    if len(stats) < rows:
        stats.append(jnp.zeros((rows - len(stats), TILE), f32))
    stats = jnp.broadcast_to(jnp.concatenate(stats, axis=0)[None], (peers, rows, TILE))
    return [stats, jnp.zeros_like(stats)] if block.shape[1] == W else [stats]


def own_products(first_ref, second_ref, out_ref, turned_ref):
    block = jnp.concatenate([first_ref[...], second_ref[...]], axis=1)
    turned = block.T
    turned_ref[...] = turned[turned_ref.shape[0] :]
    near, depth = out_ref.shape[0], out_ref.shape[1] // 2
    peers = 2 * near

    def put(at, value):
        for far in range(2):
            lo = far * depth + at
            out_ref[:, lo : lo + value.shape[1], :] = value[far * near : (far + 1) * near]

    gram = dot(turned, block)
    pack_tiles([tile_of(gram, p, q) for p, q in UPPER], block, peers, put)


def head_products(first_ref, turned_ref, next_ref, out_ref):
    block = next_ref[...]
    grams = dot(first_ref[...].T, block), dot(turned_ref[...], block)

    def put(at, value):
        out_ref[:, at : at + value.shape[1], :] = value

    half = SIDE // 2
    pack_tiles([tile_of(grams[p // half], p % half, q) for p, q in HEAD], block, out_ref.shape[0], put)


def tail_products(turned_ref, next_ref, head_ref, out_ref):
    block = next_ref[...]
    gram = dot(turned_ref[...], block)
    done = head_ref.shape[1]
    out_ref[:, :done, :] = head_ref[...]

    def put(at, value):
        out_ref[:, done + at : done + at + value.shape[1], :] = value

    half = SIDE // 2
    peers = out_ref.shape[0]
    rows = TILE // peers
    both = sums(block, peers, rows)[0][:, :SIDE]
    both = jnp.concatenate([jnp.zeros_like(both), both], axis=1).astype(i32)
    put(-rows, (both + head_ref[:, done - rows : done, :].astype(i32)).astype(i16))
    pack_tiles([tile_of(gram, p - half, q - half) for p, q in TAIL], None, peers, put)


def fold(came_ref, keep_ref, send_ref):
    near, depth = came_ref.shape[0], came_ref.shape[1] // 2
    far = lax.axis_index("cols") // near

    def total(side):
        rows = pl.ds(pl.multiple_of(side * depth, depth), depth)
        acc = came_ref[0, rows, :].astype(i32)
        for k in range(1, near):
            acc = acc + came_ref[k, rows, :].astype(i32)
        return acc

    keep_ref[...] = total(far)
    send_ref[...] = (total(1 - far) - HALF).astype(i16)


def correlate(samples, keep_ref, far_ref, next_ref, out_ref, diagonal_ref):
    peers = next_ref.shape[0]
    rows = TILE // peers
    own = keep_ref[...] + far_ref[...].astype(i32) + HALF
    nxt = next_ref[0].astype(i32)
    for k in range(1, peers):
        nxt = nxt + next_ref[k].astype(i32)
    own, nxt = own.astype(f32) / samples, nxt.astype(f32) / samples

    def stats(means):
        mean, square = means[:SIDE], means[SIDE : 2 * SIDE]
        variance = square - mean * mean
        return mean, variance, 1.0 / jnp.sqrt(jnp.maximum(variance, FLOOR))

    mean, variance, scale = stats(own[NT * rows :])
    slot = {tile: t for t, tile in enumerate(HEAD + ("sums",) + TAIL)}
    half = SIDE // 2
    at = slot["sums"] * rows
    parts = nxt[at : at + SIDE], nxt[at + SIDE : at + 2 * SIDE]
    next_mean, _, next_scale = stats(jnp.concatenate([v[k : k + half] for k in (0, half) for v in parts], axis=0))
    diagonal_ref[...] = jnp.concatenate([variance * scale * scale, jnp.zeros((8 - SIDE, TILE), f32)], axis=0)
    lane = lax.broadcasted_iota(i32, (rows, TILE), 1)
    row = lax.broadcasted_iota(i32, (rows, TILE), 0) + lax.axis_index("cols") * rows

    def at_rows(vector, p):
        return jnp.sum(jnp.where(lane == row, vector[p : p + 1], 0.0), axis=1, keepdims=True)

    row_mean = [at_rows(mean, p) for p in range(SIDE)]
    row_scale = [at_rows(scale, p) * CODE for p in range(SIDE)]

    def code(means, t, p, q, col_mean, col_scale):
        cov = means[t * rows : (t + 1) * rows] - row_mean[p] * col_mean[q : q + 1]
        return jnp.round(cov * row_scale[p] * col_scale[q : q + 1])

    upper = {(p, q): code(own, t, p, q, mean, scale) for t, (p, q) in enumerate(UPPER)}
    lower = {(p, q): code(nxt, slot[p, q], p, q, next_mean, next_scale) for p, q in LOWER}
    codes = []
    for p in range(SIDE):
        for q in range(SIDE):
            if p == q:
                codes.append(jnp.where(lane > row, upper[p, q], lower[p, q]))
            else:
                codes.append(upper[p, q] if p < q else lower[p, q])
    codes = jnp.concatenate(codes, axis=0).astype(i32).astype(i16)
    for k in range(peers):
        out_ref[k] = codes


def taper(p, q, shift):
    row = lax.broadcasted_iota(i32, (TILE, TILE), 0) + p * TILE
    col = lax.broadcasted_iota(i32, (TILE, TILE), 1) + q * TILE + shift
    reach = jnp.abs(col - row).astype(f32)
    return jnp.maximum(1.0 - reach / (W + 1), 0.0)


def unpack(codes_ref, diagonal_ref, v_ref, near_high, near_low, next_high, next_low, back_high, back_low, out_ref):
    peers = codes_ref.shape[0]
    rows = TILE // peers

    def put(high_ref, low_ref, p, q, value):
        high, low = halves(value)
        high_ref[p * TILE : (p + 1) * TILE, q * TILE : (q + 1) * TILE] = high
        low_ref[p * TILE : (p + 1) * TILE, q * TILE : (q + 1) * TILE] = low

    def put_near(p, q, code):
        value = code * (taper(p, q, 0) * (1.0 / CODE))
        if p == q:
            value = value + value.T
            value = jnp.where(on_diagonal(), diagonal_ref[p : p + 1, :], value)
            put(near_high, near_low, p, q, value)
        else:
            put(near_high, near_low, p, q, value)
            put(near_high, near_low, q, p, value.T)

    def put_next(p, q, code):
        value = code * (taper(p, q, W) * (1.0 / CODE))
        put(next_high, next_low, p, q, value)
        put(back_high, back_low, q, p, value.T)

    strict = lax.broadcasted_iota(i32, (TILE, TILE), 0) < lax.broadcasted_iota(i32, (TILE, TILE), 1)
    zero = jnp.zeros((TILE, TILE), f32)
    for p in range(SIDE):
        for u in range(SIDE // 2):
            lo = 2 * rows * (p * SIDE // 2 + u)
            pair = codes_ref[:, lo : lo + 2 * rows, :].astype(i32).astype(f32)
            for q, code in ((2 * u, pair[:, :rows]), (2 * u + 1, pair[:, rows:])):
                code = code.reshape(TILE, TILE)
                if p <= q:
                    put_near(p, q, jnp.where(strict, code, 0.0) if p == q else code)
                if p >= q:
                    put_next(p, q, code)
                else:
                    put(next_high, next_low, p, q, zero)
                    put(back_high, back_low, q, p, zero)
    encode(product(v_ref[...], next_high, next_low), out_ref)


def product(v, high_ref, low_ref):
    high, low = halves(v)
    return dot(high, high_ref[...]) + dot(low, high_ref[...]) + dot(high, low_ref[...])


def diagonal(rows):
    return lax.broadcasted_iota(i32, (rows, 256), 0) == lax.broadcasted_iota(i32, (rows, 256), 1)


def encode(v, out_ref):
    rows = v.shape[0]
    top = jnp.max(jnp.abs(v), axis=1, keepdims=True)
    power = jnp.ceil(jnp.log2(jnp.maximum(top, 1e-30)) + 0.01)
    code = jnp.round(v * (jnp.exp2(-power) * CODE))
    turned = jnp.sum(jnp.where(diagonal(rows), power, 0.0), axis=0, keepdims=True)
    tail = jnp.broadcast_to(jnp.concatenate([turned, turned], axis=1), (out_ref.shape[0] - rows, v.shape[1]))
    out_ref[...] = jnp.concatenate([code, tail], axis=0).astype(i32).astype(i16)


def decode(code, rows):
    code = code.astype(i32).astype(f32)
    power = jnp.sum(jnp.where(diagonal(rows), code[rows : rows + 1, :256], 0.0), axis=1, keepdims=True)
    return code[:rows] * (jnp.exp2(power) * (1.0 / CODE))


def start_code(v_ref, out_ref):
    encode(v_ref[...], out_ref)


def inward(v_ref, high_ref, low_ref, out_ref):
    out_ref[...] = product(v_ref[...], high_ref, low_ref) + RIDGE * v_ref[...]


def gather(part_ref, came, nxt, back_h, back_l):
    rows = part_ref.shape[0]
    return part_ref[...] + decode(came, rows) + product(decode(nxt, rows), back_h, back_l)


def first_gather(part_ref, came_ref, next_ref, back_h, back_l, next_h, next_l, out_ref, across_ref, inside_ref):
    w = gather(part_ref, came_ref[...], next_ref[...], back_h, back_l)
    hand_on(w, next_h, next_l, out_ref, across_ref, inside_ref)


def next_gather(part_ref, across_in, inside_in, back_h, back_l, next_h, next_l, out_ref, across_ref, inside_ref):
    w = gather(part_ref, *arrived(across_in, inside_in), back_h, back_l)
    hand_on(w, next_h, next_l, out_ref, across_ref, inside_ref)


def odd():
    return lax.rem(lax.axis_index("genome"), 2)


def hand_on(w, next_h, next_l, out_ref, across_ref, inside_ref):
    out_ref[...] = w

    @pl.when(odd() == 0)
    def _():
        encode(w, across_ref)
        encode(product(w, next_h, next_l), inside_ref)

    @pl.when(odd() == 1)
    def _():
        encode(product(w, next_h, next_l), across_ref)
        encode(w, inside_ref)


def arrived(across_in, inside_in):
    even = odd() == 0
    across, inside = across_in[...].astype(i32), inside_in[...].astype(i32)
    return jnp.where(even, across, inside), jnp.where(even, inside, across)


def along(a, b):
    return jnp.sum(a * b, axis=1, keepdims=True)


def turn(moment):
    return jnp.sum(jnp.where(diagonal(moment.shape[0]), moment, 0.0), axis=0, keepdims=True)


def early_moments(a_ref, b_ref, c_ref, out_ref):
    a, b, c = a_ref[...], b_ref[...], c_ref[...]
    rows = [turn(m) for m in (along(a, a), along(a, b), along(b, b), along(b, c), along(c, c))]
    out_ref[...] = jnp.concatenate(rows + [jnp.zeros((3, 256), f32)], axis=0)


def last_vector(part_ref, across_in, inside_in, back_h, back_l, c_ref, early_ref, out_ref, moments_ref):
    w = gather(part_ref, *arrived(across_in, inside_in), back_h, back_l)
    out_ref[...] = w
    early = early_ref[...]
    rows = [early[k : k + 1, :SLOT] for k in range(5)] + [turn(along(c_ref[...], w))[:, :SLOT]]
    fill = moments_ref.shape[2] - 6 * SLOT
    moments = jnp.concatenate(rows + [jnp.zeros((1, fill), f32)], axis=1)
    for k in range(moments_ref.shape[0]):
        moments_ref[k] = moments


def combine(moments_ref, a_ref, b_ref, c_ref, d_ref, effects_ref, residual_ref):
    total = moments_ref[0]
    for k in range(1, moments_ref.shape[0]):
        total = total + moments_ref[k]
    first = total[:, :256]
    moment = [total[:, k * SLOT : k * SLOT + 256] / first for k in range(6)]

    def inner(x, y, power):
        return sum(
            x[i] * y[j] * moment[i + j + power] for i in range(len(x)) for j in range(len(y))
        )

    one = jnp.ones_like(moment[0])
    residual, direction, effects = [one], [one], []
    norm_now = inner(residual, residual, 0)
    for step in range(3):
        step_size = norm_now / inner(direction, direction, 1)
        effects = [
            (effects[k] if k < len(effects) else 0.0) + step_size * direction[k] for k in range(len(direction))
        ]
        image = [0.0] + direction
        residual = [
            (residual[k] if k < len(residual) else 0.0) - step_size * image[k] for k in range(len(image))
        ]
        if step < 2:
            norm_next = inner(residual, residual, 0)
            ratio = norm_next / norm_now
            direction = [
                residual[k] + (ratio * direction[k] if k < len(direction) else 0.0) for k in range(len(residual))
            ]
            norm_now = norm_next
    rows = effects + residual
    table = jnp.concatenate(rows + [jnp.zeros((TILE - len(rows), 256), f32)], axis=0).T
    table = table[: a_ref.shape[0]]
    col = [table[:, k : k + 1] for k in range(len(rows))]
    a, b, c, d = a_ref[...], b_ref[...], c_ref[...], d_ref[...]
    effects_ref[...] = col[0] * a + col[1] * b + col[2] * c
    residual_ref[...] = col[3] * a + col[4] * b + col[5] * c + col[6] * d


def shards(genotypes, z_scores):
    local_samples, variants = genotypes.shape
    blocks = lax.axis_size("genome")
    peers = lax.axis_size("cols")
    samples = local_samples * peers
    to_left = [(k + 1, k) for k in range(blocks - 1)]
    to_right = [(k, k + 1) for k in range(blocks - 1)]
    rows = TILE // peers

    near = peers // 2
    depth = NT * rows + 16
    cols = range(peers)
    sides = [list(cols[:near]), list(cols[near:])]

    half = variants // 2
    first = genotypes[:, :half].astype(bf16)
    next_first = lax.ppermute(first, "genome", to_left)
    second = lax.optimization_barrier((genotypes, first))[0][:, half:].astype(bf16)
    next_second = lax.ppermute(second, "genome", to_left)
    own, turned = call(
        own_products,
        (jax.ShapeDtypeStruct((near, 2 * depth, TILE), i16), shape(half, local_samples, dtype=bf16)),
        first,
        second,
    )
    own = lax.all_to_all(own, "cols", 0, 0, axis_index_groups=sides)
    head = call(head_products, shape(peers, 8 * rows, TILE, dtype=i16), first, turned, next_first)
    keep, far = call(fold, (shape(depth, TILE, dtype=i32), shape(depth, TILE, dtype=i16)), own)
    z = z_scores.T
    vector = shape(*z.shape)
    code = shape(z.shape[0] // 16 * 16 + 16, z.shape[1], dtype=i16)
    z_code = call(start_code, code, z)
    far = lax.ppermute(far, "cols", [(k, (k + near) % peers) for k in cols])
    nxt = call(tail_products, shape(peers, (NT + 1) * rows, TILE, dtype=i16), turned, next_second, head)
    nxt = lax.all_to_all(nxt, "cols", 0, 0)
    z_next = lax.ppermute(z_code, "genome", to_left)
    codes, diagonal_row = call(
        functools.partial(correlate, samples),
        (shape(peers, SIDE * SIDE * rows, TILE, dtype=i16), shape(8, TILE)),
        keep,
        far,
        nxt,
    )
    codes, z_next = lax.optimization_barrier((codes, z_next))
    codes = lax.all_to_all(codes, "cols", 0, 0)
    square = shape(W, W, dtype=bf16)
    near_h, near_l, next_h, next_l, back_h, back_l, out = call(unpack, (square,) * 6 + (code,), codes, diagonal_row, z)

    inside = [(k, k ^ 1) for k in range(blocks)]
    across = [(k, ((k + 1) ^ 1) - 1) for k in range(1, blocks - 1)]

    def step(kernel, part, *came):
        w, out, inn = call(
            kernel, (vector, code, code), part, *came, back_h, back_l, next_h, next_l
        )
        out = lax.ppermute(out, "genome", across)
        inn = lax.ppermute(inn, "genome", inside)
        return w, call(inward, vector, w, near_h, near_l), out, inn

    came = lax.ppermute(out, "genome", to_right)
    one, *rest = step(first_gather, call(inward, vector, z, near_h, near_l), came, z_next)
    two, part, out, inn = step(next_gather, *rest)
    early = call(early_moments, shape(8, 256), z, one, two)
    three, moments = call(
        last_vector, (vector, shape(blocks, 1, 1280)), part, out, inn, back_h, back_l, two, early
    )
    moments = lax.all_to_all(moments, "genome", 0, 0)
    effects, residual = call(combine, (jax.ShapeDtypeStruct(z.shape, f32),) * 2, moments, z, one, two, three)
    return effects.T, residual.T


def solution(mesh):
    return jax.shard_map(
        shards,
        mesh=mesh,
        in_specs=(P("cols", "genome"), P("genome", "cols")),
        out_specs=(P("genome", "cols"), P("genome", "cols")),
        check_vma=False,
    )
```
